512 devices in a mesh: wide: 64 (over z, y_hi, core), narrow: 8 (over y_lo, x).
Axes of the slice: x: 4, y: 4 (y_hi: 2, y_lo: 2; y = y_hi * 2 + y_lo), z: 16, core: 2. Of those that a mesh axis runs over, the one named last changes fastest.
Arguments:
- offsets: float32 [3, 64, 8, 512], P(None, 'wide', 'narrow'), may hold values from 0 to 1
- bases: int32 [3, 64, 8, 512], P(None, 'wide', 'narrow'), may hold values from 0 to 511, as said below
- charges: float32 [64, 8, 512], P('wide', 'narrow'), may hold values from -4 to 4
- counts: int32 [64, 8], P('wide', 'narrow'), may hold values from 32 to 512, as said below
- cotangent: float32 [1], replicated, may hold values from 0.5 to 2
Outputs:
- forces: float32 [3, 64, 8, 512], P(None, 'wide', 'narrow')
- charge_grads: float32 [64, 8, 512], P('wide', 'narrow')
The draws below stay inside these ranges and needn't reach their ends.
Inputs may be any that keep to these rules, and one draw needn't show every extreme that they name: `counts`: slots at or beyond a domain's count are padding; some domain holds exactly 512 atoms. `bases`: component 0 is below 4 and component 1 below 8 (the lowest stencil cell lies in the atom's own domain); component 2 is below 512.
All inputs are finite; a program needn't handle non-finite values.
Results may differ from the reference program's by a relative error of at most 0.0003.
Values sent between devices are 32-bit elements; how exact they have to be, the bound alone decides.
A program may use at most 64 MiB of HBM per device.

```python
import math
import jax
import jax.numpy as jnp

CX = 4
CY = 8
NZ = 512
CAP = 512
DOMAINS_X = 64
DOMAINS_Y = 8
N_WIDE = 64
N_NARROW = 8


def draw_counts(key, part):
    key_shift, key_dense, key_sparse, key_row = jax.random.split(key, 4)
    wide_ids = jnp.arange(DOMAINS_X, dtype=jnp.int32)[:, None]
    narrow_ids = jnp.arange(DOMAINS_Y, dtype=jnp.int32)[None, :]
    liquid_start = jax.random.randint(key_shift, (), 0, DOMAINS_X)
    liquid = (wide_ids - liquid_start) % DOMAINS_X < max(DOMAINS_X // 4, 1)
    dense = CAP - jax.random.randint(key_dense, (DOMAINS_X, DOMAINS_Y), 0, CAP // 8)
    sparse = jax.random.randint(key_sparse, (DOMAINS_X, DOMAINS_Y), CAP // 16, CAP // 8)
    full_row = jax.random.randint(key_row, (), 0, DOMAINS_Y)
    filled = (wide_ids == liquid_start) & (narrow_ids == full_row)
    return jnp.where(filled, CAP, jnp.where(liquid, dense, sparse)).astype(jnp.int32)


def draw_bases(key, part):
    key_first, key_second, key_third = jax.random.split(key, 3)
    shape = (DOMAINS_X, DOMAINS_Y, CAP)
    first = jax.random.randint(key_first, shape, 0, CX)
    second = jax.random.randint(key_second, shape, 0, CY)
    third = jax.random.randint(key_third, shape, 0, NZ)
    return jnp.stack([first, second, third]).astype(jnp.int32)


def block_scale(rng, extent, cuts, low, top_value):
    gain = 1.0
    for dim, blocks in cuts:
        draws = jax.random.uniform(jax.random.fold_in(jax.random.fold_in(rng, 6), dim), (blocks,), jnp.float32, low / len(cuts), top_value / len(cuts))
        gain = gain * jnp.repeat(jnp.exp(draws), extent[dim] // blocks).reshape((-1,) + (1,) * (len(extent) - 1 - dim))
    return gain


def noise(rng, shape, spread, limit, cuts=(), held_as=jnp.bfloat16):
    level = block_scale(rng, shape, cuts, -0.22, 0.18) if cuts else 1.0
    result = jax.random.normal(rng, shape, jnp.float32) * spread * level
    return jnp.minimum(jnp.maximum(result, -limit), limit).astype(held_as)


def setup_inputs(seed: int = 0) -> dict:
    arg_keys = jax.random.split(jax.random.key(seed), 6)
    return {
        "offsets": jnp.clip(1.0 * jax.random.uniform(arg_keys[0], (3, DOMAINS_X, DOMAINS_Y, CAP), jnp.float32) ** block_scale(arg_keys[0], (3, DOMAINS_X, DOMAINS_Y, CAP), ((1, 64), (2, 8)), -0.2, 0.2), 0.0, 1.0),
        "bases": draw_bases(jax.random.fold_in(arg_keys[5], 71), 0),
        "charges": noise(arg_keys[2], (DOMAINS_X, DOMAINS_Y, CAP), 1.0, 4.0, ((0, 64), (1, 8)), jnp.float32),
        "counts": draw_counts(jax.random.fold_in(arg_keys[5], 71), 0),
        "cotangent": jnp.clip(jax.random.uniform(arg_keys[4], (1,), jnp.float32, 0.5, 2.0), 0.5, 2.0),
    }


splitting_width = 1.0


def spline_pair(offset):
    rest = 1.0 - offset
    square = offset * offset
    cube = square * offset
    weights = jnp.stack([rest * rest * rest / 6.0, (3.0 * cube - 6.0 * square + 4.0) / 6.0,
                         (-3.0 * cube + 3.0 * square + 3.0 * offset + 1.0) / 6.0, cube / 6.0], axis=1)
    slopes = jnp.stack([-0.5 * rest * rest, 1.5 * square - 2.0 * offset,
                        -1.5 * square + offset + 0.5, 0.5 * square], axis=1)
    return weights, slopes


def wave_terms(wave_index, length):
    signed = jnp.where(2 * wave_index < length, wave_index, wave_index - length).astype(jnp.float32) / length
    phase_angle = (wave_index % length).astype(jnp.float32) * (2.0 * math.pi / length)
    spline = 9.0 / (2.0 + jnp.cos(phase_angle)) ** 2
    return signed * signed, spline


def influence(wave_x, wave_y, wave_z, size_x, size_y, size_z):
    square_x, spline_x = wave_terms(wave_x, size_x)
    square_y, spline_y = wave_terms(wave_y, size_y)
    square_z, spline_z = wave_terms(wave_z, size_z)
    squared = square_x + square_y + square_z
    positive = jnp.where(squared > 0.0, squared, 1.0)
    volume = float(size_x * size_y * size_z)
    kernel = jnp.exp(-(math.pi ** 2) * squared / (splitting_width * splitting_width)) / (math.pi * volume * positive)
    kernel = kernel * spline_x * spline_y * spline_z
    return jnp.where(squared > 0.0, kernel, 0.0)


def reference(offsets, bases, charges, counts, cotangent):
    size_x = CX * N_WIDE
    size_y = CY * N_NARROW
    size_z = NZ
    occupied = (jnp.arange(CAP, dtype=jnp.int32)[None, None, :] < counts[:, :, None]).astype(jnp.float32)
    charge = charges * occupied
    weights, slopes = spline_pair(offsets)
    stencil = jnp.arange(4, dtype=jnp.int32)[:, None, None, None]
    cell_x = (bases[0][None] + CX * jnp.arange(DOMAINS_X, dtype=jnp.int32)[None, :, None, None] + stencil) % size_x
    cell_y = (bases[1][None] + CY * jnp.arange(DOMAINS_Y, dtype=jnp.int32)[None, None, :, None] + stencil) % size_y
    cell_z = (bases[2][None] + stencil) % size_z
    plane_places = cell_y[:, None] * size_z + cell_z[None, :]
    weight_yz = weights[1][:, None] * weights[2][None, :]
    flat_grid = jnp.zeros((size_x * size_y * size_z,), jnp.float32)
    for offset_x in range(4):
        places = cell_x[offset_x][None, None] * (size_y * size_z) + plane_places
        amounts = weights[0][offset_x][None, None] * weight_yz * charge[None, None]
        flat_grid = flat_grid.at[places.reshape(-1)].add(amounts.reshape(-1))
    spectrum = jnp.fft.fftn(flat_grid.reshape(size_x, size_y, size_z))
    kernel = influence(jnp.arange(size_x, dtype=jnp.int32)[:, None, None],
                       jnp.arange(size_y, dtype=jnp.int32)[None, :, None],
                       jnp.arange(size_z, dtype=jnp.int32)[None, None, :], size_x, size_y, size_z)
    potential = (jnp.real(jnp.fft.ifftn(spectrum * kernel)) * float(size_x * size_y * size_z)).astype(jnp.float32)
    potential = potential.reshape(-1)
    factor = cotangent[0]
    slope_yz_y = slopes[1][:, None] * weights[2][None, :]
    slope_yz_z = weights[1][:, None] * slopes[2][None, :]
    potential_sum = jnp.zeros_like(charges)
    pull_x = jnp.zeros_like(charges)
    pull_y = jnp.zeros_like(charges)
    pull_z = jnp.zeros_like(charges)
    for offset_x in range(4):
        places = cell_x[offset_x][None, None] * (size_y * size_z) + plane_places
        nearby = potential[places]
        in_plane = jnp.sum(weight_yz * nearby, axis=(0, 1))
        potential_sum = potential_sum + weights[0][offset_x] * in_plane
        pull_x = pull_x + slopes[0][offset_x] * in_plane
        pull_y = pull_y + weights[0][offset_x] * jnp.sum(slope_yz_y * nearby, axis=(0, 1))
        pull_z = pull_z + weights[0][offset_x] * jnp.sum(slope_yz_z * nearby, axis=(0, 1))
    charge_grads = factor * occupied * potential_sum
    forces = -factor * charge[None] * jnp.stack([pull_x, pull_y, pull_z])
    return forces, charge_grads
```

```python
import math

import jax
import jax.numpy as jnp
import ml_dtypes
import numpy as np
from jax import lax
from jax.experimental import pallas as pl
from jax.experimental.pallas import tpu as pltpu
from jax.sharding import PartitionSpec as P

CX = 4
CY = 8
NZ = 512
WIDE = 64
NARROW = 8
NX = CX * WIDE
NY = CY * NARROW
SLOTS = 512
ROWS = 24
HALF = 64
MESH = pl.DeviceIdType.MESH
VMEM = pltpu.VMEM
F32 = jnp.float32
BF16 = jnp.bfloat16


def real_basis(length):
    c = np.arange(length)
    freq = np.where(c <= length // 2, c, length - c)
    phase = (freq[:, None] * c[None, :]) % length * (2.0 * np.pi / length)
    scale = np.where((freq == 0) | (2 * freq == length), 1.0, np.sqrt(2.0)) / np.sqrt(length)
    table = np.where((c <= length // 2)[:, None], np.cos(phase), np.sin(phase)) * scale[:, None]
    return table, freq


def halves(table):
    table = np.asarray(table, np.float32)
    high = table.astype(ml_dtypes.bfloat16)
    low = (table - high.astype(np.float32)).astype(ml_dtypes.bfloat16)
    return high, low


def frequency_factors(length):
    freq = real_basis(length)[1]
    square = (freq / length) ** 2
    spline = 9.0 / (2.0 + np.cos(2.0 * np.pi * freq / length)) ** 2
    return square, np.exp(-(np.pi**2) * square) * spline


def row_matrix():
    basis = real_basis(NY)[0]
    i = np.arange(ROWS)
    row = np.where(i < 16, i % 8, 8 + i % 4)
    parity = np.where(i < 16, i // 8, (i // 4) % 2)
    table = np.zeros((NARROW, ROWS, 2, NY))
    for n in range(NARROW):
        for j in range(ROWS):
            if row[j] < CY + 3:
                table[n, j, parity[j]] = basis[:, (CY * n + row[j]) % NY]
    return table.reshape(NARROW * ROWS, 2 * NY)


def split(value):
    high = value.astype(BF16)
    return high, (value - high.astype(F32)).astype(BF16)


def dot3(a, b, contract):
    dims = (contract, ((), ()))

    def one(x, y):
        return lax.dot_general(x, y, dims, preferred_element_type=F32)

    return one(a[0], b[0]) + (one(a[0], b[1]) + one(a[1], b[0]))


def pick(steps, values):
    out = jnp.where(steps == 3, values[3], 0.0)
    for j in (2, 1, 0):
        out = jnp.where(steps == j, values[j], out)
    return out


def spline_weights(t):
    s = 1.0 - t
    square = t * t
    cube = square * t
    return (
        s * s * s / 6.0,
        (3.0 * cube - 6.0 * square + 4.0) / 6.0,
        (-3.0 * cube + 3.0 * square + 3.0 * t + 1.0) / 6.0,
        cube / 6.0,
    )


def spline_slopes(t):
    s = 1.0 - t
    square = t * t
    return (-0.5 * s * s, 1.5 * square - 2.0 * t, -1.5 * square + t + 0.5, 0.5 * square)


def swap(value):
    return pltpu.roll(value, HALF, 1)


def kernel(
    count_ref,
    factor_ref,
    zsquare_ref,
    zgain_ref,
    offset_ref,
    base_ref,
    charge_ref,
    zh_ref,
    zl_ref,
    yh_ref,
    yl_ref,
    yth_ref,
    ytl_ref,
    xh_ref,
    xl_ref,
    xth_ref,
    xtl_ref,
    gain_ref,
    square_ref,
    force_ref,
    grad_ref,
    send_a,
    recv_a,
    send_b,
    recv_b,
    send_c,
    recv_c,
    send_d,
    recv_d,
    depth_h,
    depth_l,
    slope_h,
    slope_l,
    send_sems,
    recv_sems,
):
    w = lax.axis_index("wide")
    n = lax.axis_index("narrow")
    above = lax.rem(w + 1, WIDE)
    below = lax.rem(w + WIDE - 1, WIDE)

    barrier = pltpu.get_barrier_semaphore()

    def greet(to):
        pl.semaphore_signal(barrier, inc=1, device_id=to, device_id_type=MESH)

    def greet_wide(i, carry):
        greet((lax.rem(w + i, WIDE), n))
        return carry

    def greet_narrow(i, carry):
        other = lax.rem(n + i, NARROW)
        greet((w, other))
        greet((above, other))
        greet((below, other))
        return carry

    lax.fori_loop(1, NARROW, greet_narrow, 0)
    lax.fori_loop(1, WIDE, greet_wide, 0)

    low_lanes = lax.broadcasted_iota(jnp.int32, (1, 128), 1) < HALF

    t = [offset_ref[d : d + 1, :] for d in range(3)]
    corner = [base_ref[d : d + 1, :] for d in range(3)]
    weights = [spline_weights(v) for v in t]
    slopes = [spline_slopes(v) for v in t]
    occupied = lax.broadcasted_iota(jnp.int32, (1, SLOTS), 1) < count_ref[0, 0]
    charge = jnp.where(occupied, charge_ref[...], 0.0)

    def depth_steps(first):
        cell = lax.broadcasted_iota(jnp.int32, (128, SLOTS), 0) + first
        return (cell - corner[2]) & (NZ - 1)

    for first in range(0, NZ, 128):
        high, low = split(pick(depth_steps(first), weights[2]))
        depth_h[first : first + 128, :] = high
        depth_l[first : first + 128, :] = low

    index = lax.broadcasted_iota(jnp.int32, (ROWS, SLOTS), 0)
    row = jnp.where(index < 16, index & 7, 8 + (index & 3))
    parity = jnp.where(index < 16, index >> 3, (index >> 2) & 1)
    row_steps = row - corner[1]
    row_w = pick(row_steps, weights[1])
    row_s = pick(row_steps, slopes[1])
    plane_steps = [parity + 2 * g - corner[0] for g in range(4)]
    row_q = row_w * charge
    cross = jnp.concatenate([row_q * pick(plane_steps[g], weights[0]) for g in range(4)], axis=0)
    grid = dot3(split(cross), (depth_h[...], depth_l[...]), ((1,), (1,)))
    spectrum = dot3(split(grid), (zh_ref[...], zl_ref[...]), ((1,), (0,)))
    for side in range(2):
        for m in range(4):
            lanes = slice(128 * m, 128 * m + 128)
            first = spectrum[ROWS * 2 * side : ROWS * (2 * side + 1), lanes]
            second = spectrum[ROWS * (2 * side + 1) : ROWS * (2 * side + 2), lanes]
            send_a[8 * side + 2 * m] = jnp.where(low_lanes, first, swap(second))
            send_a[8 * side + 2 * m + 1] = jnp.where(low_lanes, swap(first), second)

    pl.semaphore_wait(barrier, 3 * (NARROW - 1) + WIDE - 1)

    def push(stage, source, target, to):
        pltpu.make_async_remote_copy(
            src_ref=source,
            dst_ref=target,
            send_sem=send_sems.at[stage],
            recv_sem=recv_sems.at[stage],
            device_id=to,
            device_id_type=MESH,
        ).start()

    def drain(stage, block):
        return pltpu.make_async_remote_copy(
            src_ref=block,
            dst_ref=block,
            send_sem=send_sems.at[stage],
            recv_sem=recv_sems.at[stage],
            device_id=(w, n),
            device_id_type=MESH,
        )

    def push_a(i, carry):
        other = lax.rem(n + i, NARROW)
        push(0, send_a.at[other], recv_a.at[n], (w, other))
        push(0, send_a.at[8 + other], recv_a.at[8 + n], (above, other))
        return carry

    push(0, send_a.at[8 + n], recv_a.at[8 + n], (above, n))
    lax.fori_loop(1, NARROW, push_a, 0)
    recv_a[n] = send_a[n]

    for first in range(0, NZ, 128):
        high, low = split(pick(depth_steps(first), slopes[2]))
        slope_h[first : first + 128, :] = high
        slope_l[first : first + 128, :] = low
    coefficient = HALF * n + w
    squared = square_ref[...] + zsquare_ref[0, coefficient]
    positive = jnp.where(squared > 0.0, squared, 1.0)
    influence = jnp.where(squared > 0.0, gain_ref[...] * zgain_ref[0, coefficient] / positive, 0.0)

    drain(0, recv_a.at[pl.ds(0, 15)]).wait_recv()
    rows = recv_a[0:8] + recv_a[8:16]
    rows = rows.reshape(NARROW * ROWS, 128)
    columns = dot3((yth_ref[...], ytl_ref[...]), split(rows), ((1,), (0,)))
    columns = columns.T
    send_b[pl.ds(0, HALF, 2), :] = columns[:HALF]
    send_b[pl.ds(1, HALF, 2), :] = columns[HALF:]

    def push_b(i, carry):
        other = lax.rem(w + i, WIDE)
        push(1, send_b.at[pl.ds(2 * other, 2)], recv_b.at[pl.ds(2 * w, 2)], (other, n))
        return carry

    lax.fori_loop(1, WIDE, push_b, 0)
    recv_b[pl.ds(2 * w, 2), :] = send_b[pl.ds(2 * w, 2), :]
    drain(1, recv_b.at[pl.ds(0, 2 * WIDE - 2)]).wait_recv()

    planes = recv_b[...]
    turned = swap(planes)
    stacked = jnp.concatenate(
        [jnp.where(low_lanes, planes, turned), jnp.where(low_lanes, turned, planes)], axis=0
    )
    filtered = dot3((xh_ref[...], xl_ref[...]), split(stacked), ((1,), (0,))) * influence
    planes = dot3((xth_ref[...], xtl_ref[...]), split(filtered), ((1,), (0,)))
    send_c[...] = jnp.where(low_lanes, planes[:128], planes[128:])

    def push_c(i, carry):
        other = lax.rem(w + i, WIDE)
        push(2, send_c.at[pl.ds(2 * other, 2)], recv_c.at[pl.ds(2 * w, 2)], (other, n))
        return carry

    lax.fori_loop(1, WIDE, push_c, 0)
    recv_c[pl.ds(2 * w, 2), :] = send_c[pl.ds(2 * w, 2), :]
    drain(2, recv_c.at[pl.ds(0, 2 * WIDE - 2)]).wait_recv()

    columns = jnp.concatenate(
        [recv_c[pl.ds(0, HALF, 2), :], recv_c[pl.ds(1, HALF, 2), :]], axis=0
    )
    rows = dot3((yh_ref[...], yl_ref[...]), split(columns), ((1,), (1,)))
    send_d[...] = rows.reshape(NARROW, ROWS, 128)

    def push_d(i, carry):
        other = lax.rem(n + i, NARROW)
        push(3, send_d.at[other], recv_d.at[n], (w, other))
        push(3, send_d.at[other], recv_d.at[8 + n], (below, other))
        return carry

    push(3, send_d.at[n], recv_d.at[8 + n], (below, n))
    lax.fori_loop(1, NARROW, push_d, 0)
    recv_d[n] = send_d[n]
    drain(3, recv_d.at[pl.ds(0, 15)]).wait_recv()

    groups = []
    for side in range(2):
        tiles = [recv_d[8 * side + m] for m in range(8)]
        pairs = [(tiles[2 * m], tiles[2 * m + 1]) for m in range(4)]
        groups.append(jnp.concatenate([jnp.where(low_lanes, a, swap(b)) for a, b in pairs], axis=1))
        groups.append(jnp.concatenate([jnp.where(low_lanes, swap(a), b) for a, b in pairs], axis=1))
    spectrum = jnp.concatenate(groups, axis=0)
    potential = split(dot3(split(spectrum), (zh_ref[...], zl_ref[...]), ((1,), (1,))))
    along_w = dot3(potential, (depth_h[...], depth_l[...]), ((1,), (0,)))
    along_s = dot3(potential, (slope_h[...], slope_l[...]), ((1,), (0,)))

    total = jnp.zeros((ROWS, SLOTS), F32)
    pull_x, pull_y, pull_z = total, total, total
    for g in range(4):
        part = slice(ROWS * g, ROWS * g + ROWS)
        plane_w = pick(plane_steps[g], weights[0])
        plane_s = pick(plane_steps[g], slopes[0])
        weighted = along_w[part] * plane_w
        total = total + weighted
        pull_x = pull_x + along_w[part] * plane_s
        pull_z = pull_z + along_s[part] * plane_w

    def over_rows(value):
        return jnp.sum(value, axis=0, keepdims=True)

    factor = factor_ref[0]
    pull_y = over_rows(total * row_s)
    total = over_rows(total * row_w)
    pull_x = over_rows(pull_x * row_w)
    pull_z = over_rows(pull_z * row_w)
    grad_ref[...] = jnp.where(occupied, factor * total, 0.0)
    pull = -factor * charge
    force_ref[0:1, :] = pull * pull_x
    force_ref[1:2, :] = pull * pull_y
    force_ref[2:3, :] = pull * pull_z

    drain(0, recv_a.at[pl.ds(0, 15)]).wait_send()
    drain(1, recv_b.at[pl.ds(0, 2 * WIDE - 2)]).wait_send()
    drain(2, recv_c.at[pl.ds(0, 2 * WIDE - 2)]).wait_send()
    drain(3, recv_d.at[pl.ds(0, 15)]).wait_send()


def on_device(offsets, bases, charges, counts, cotangent):
    z_table = halves(real_basis(NZ)[0].T)
    y_table = row_matrix()
    y_pair = halves(y_table)
    y_turned = halves(y_table.T)
    x_basis = real_basis(NX)[0]
    x_table = np.concatenate([x_basis[:, 0::2], x_basis[:, 1::2]], axis=1)
    x_pair = halves(x_table)
    x_turned = halves(x_table.T)
    square_x, gain_x = frequency_factors(NX)
    square_y, gain_y = frequency_factors(NY)
    square_z, gain_z = frequency_factors(NZ)
    square = (square_x[:, None] + np.tile(square_y, 2)[None, :]).astype(np.float32)
    gain = (gain_x[:, None] * np.tile(gain_y, 2)[None, :] / math.pi).astype(np.float32)
    scalars = pl.BlockSpec(memory_space=pltpu.SMEM)
    arrays = pl.BlockSpec(memory_space=VMEM)
    forces, grads = pl.pallas_call(
        kernel,
        out_shape=(
            jax.ShapeDtypeStruct((3, SLOTS), F32),
            jax.ShapeDtypeStruct((1, SLOTS), F32),
        ),
        in_specs=[scalars] * 4 + [arrays] * 15,
        out_specs=(arrays, arrays),
        scratch_shapes=[
            VMEM((2 * NARROW, ROWS, 128), F32),
            VMEM((2 * NARROW, ROWS, 128), F32),
            VMEM((2 * WIDE, 128), F32),
            VMEM((2 * WIDE, 128), F32),
            VMEM((2 * WIDE, 128), F32),
            VMEM((2 * WIDE, 128), F32),
            VMEM((NARROW, ROWS, 128), F32),
            VMEM((2 * NARROW, ROWS, 128), F32),
            VMEM((NZ, SLOTS), BF16),
            VMEM((NZ, SLOTS), BF16),
            VMEM((NZ, SLOTS), BF16),
            VMEM((NZ, SLOTS), BF16),
            pltpu.SemaphoreType.DMA((4,)),
            pltpu.SemaphoreType.DMA((4,)),
        ],
        compiler_params=pltpu.CompilerParams(
            collective_id=0, has_side_effects=True, vmem_limit_bytes=40 * 1024 * 1024
        ),
        name="ewald",
    )(
        counts,
        cotangent,
        square_z.astype(np.float32).reshape(1, NZ),
        gain_z.astype(np.float32).reshape(1, NZ),
        offsets.reshape(3, SLOTS),
        bases.reshape(3, SLOTS),
        charges.reshape(1, SLOTS),
        *z_table,
        *y_pair,
        *y_turned,
        *x_pair,
        *x_turned,
        gain,
        square,
    )
    return forces.reshape(3, 1, 1, SLOTS), grads.reshape(1, 1, SLOTS)


def solution(mesh):
    placed = (
        P(None, "wide", "narrow", None),
        P(None, "wide", "narrow", None),
        P("wide", "narrow", None),
        P("wide", "narrow"),
        P(),
    )
    return jax.shard_map(
        on_device,
        mesh=mesh,
        in_specs=placed,
        out_specs=(P(None, "wide", "narrow", None), P("wide", "narrow", None)),
        check_vma=False,
    )
```

```python
import math

import jax
import jax.numpy as jnp
import ml_dtypes
import numpy as np
from jax import lax
from jax.experimental import pallas as pl
from jax.experimental.pallas import tpu as pltpu
from jax.sharding import PartitionSpec as P

CX = 4
CY = 8
NZ = 512
WIDE = 64
NARROW = 8
NX = CX * WIDE
NY = CY * NARROW
SLOTS = 512
ROWS = CY + 3
RING = 16
DOMAINS = WIDE // RING
PLANES = CX + 3
HALF = 64
MESH = pl.DeviceIdType.MESH
VMEM = pltpu.VMEM
F32 = jnp.float32
BF16 = jnp.bfloat16


def real_basis(length):
    c = np.arange(length)
    freq = np.where(c <= length // 2, c, length - c)
    phase = (freq[:, None] * c[None, :]) % length * (2.0 * np.pi / length)
    scale = np.where((freq == 0) | (2 * freq == length), 1.0, np.sqrt(2.0)) / np.sqrt(length)
    table = np.where((c <= length // 2)[:, None], np.cos(phase), np.sin(phase)) * scale[:, None]
    return table, freq


def halves(table):
    table = np.asarray(table, np.float32)
    high = table.astype(ml_dtypes.bfloat16)
    low = (table - high.astype(np.float32)).astype(ml_dtypes.bfloat16)
    return high, low


def frequency_factors(length):
    freq = real_basis(length)[1]
    square = (freq / length) ** 2
    spline = 9.0 / (2.0 + np.cos(2.0 * np.pi * freq / length)) ** 2
    return square, np.exp(-(np.pi**2) * square) * spline


def row_matrix():
    basis = real_basis(NY)[0]
    table = np.zeros((2, NARROW, ROWS, 2, NY))
    for half in range(2):
        for n in range(NARROW):
            for r in range(ROWS):
                table[half, n, r, half] = basis[:, (CY * n + r) % NY]
    return table.reshape(2 * NARROW * ROWS, 2 * NY)


def plane_order():
    half, place, other, plane = np.meshgrid(
        np.arange(2), np.arange(RING), np.arange(2), np.arange(CX), indexing="ij"
    )
    return (CX * (DOMAINS * place + 2 * other + half) + plane).reshape(-1)


def split(value):
    high = value.astype(BF16)
    return high, (value - high.astype(F32)).astype(BF16)


def dot3(a, b, contract):
    dims = (contract, ((), ()))

    def one(x, y):
        return lax.dot_general(x, y, dims, preferred_element_type=F32)

    return one(a[0], b[0]) + (one(a[0], b[1]) + one(a[1], b[0]))


def pick(steps, values):
    out = jnp.where(steps == 3, values[3], 0.0)
    for j in (2, 1, 0):
        out = jnp.where(steps == j, values[j], out)
    return out


def spline_weights(t):
    s = 1.0 - t
    square = t * t
    cube = square * t
    return (
        s * s * s / 6.0,
        (3.0 * cube - 6.0 * square + 4.0) / 6.0,
        (-3.0 * cube + 3.0 * square + 3.0 * t + 1.0) / 6.0,
        cube / 6.0,
    )


def spline_slopes(t):
    s = 1.0 - t
    square = t * t
    return (-0.5 * s * s, 1.5 * square - 2.0 * t, -1.5 * square + t + 0.5, 0.5 * square)


def swap(value):
    return pltpu.roll(value, HALF, 1)


def exchange_lanes(blocks, lanes):
    blocks = list(blocks)
    for bit in range(3):
        step = 1 << bit
        clear = (lanes & step) == 0
        for a in range(8):
            if not a & step:
                x, y = blocks[a], blocks[a + step]
                blocks[a] = jnp.where(clear, x, pltpu.roll(y, step, 1))
                blocks[a + step] = jnp.where(clear, pltpu.roll(x, 128 - step, 1), y)
    return blocks


def far_first(sizes):
    offsets = [o for o in np.ndindex(*sizes) if any(o)]

    def hops(offset):
        return sum(min(o, size - o) for o, size in zip(offset, sizes))

    return sorted(offsets, key=lambda o: -hops(o))


def kernel(
    count_hbm,
    factor_hbm,
    offset_hbm,
    base_hbm,
    charge_hbm,
    zh_hbm,
    zl_hbm,
    yh_hbm,
    yl_hbm,
    yth_hbm,
    ytl_hbm,
    xh_hbm,
    xl_hbm,
    xth_hbm,
    xtl_hbm,
    gain_hbm,
    square_hbm,
    zfactor_hbm,
    force_ref,
    grad_ref,
    count_ref,
    factor_ref,
    offset_ref,
    base_ref,
    charge_ref,
    zh_ref,
    zl_ref,
    yh_ref,
    yl_ref,
    yth_ref,
    ytl_ref,
    xh_ref,
    xl_ref,
    xth_ref,
    xtl_ref,
    gain_ref,
    square_ref,
    zfactor_ref,
    send_a,
    recv_a,
    send_b,
    recv_b,
    send_c,
    recv_c,
    send_d,
    recv_d,
    depth_h,
    depth_l,
    slope_h,
    slope_l,
    send_sems,
    recv_sems,
    local_sems,
):
    w = lax.axis_index("wide")
    n = lax.axis_index("narrow")
    place = w // DOMAINS
    v = w % DOMAINS
    core = v % 2
    y = (v // 2) * 2 + n // 4
    x = n % 4

    def ring_mate(offset):
        other = (place + offset) % RING
        return other, (other * DOMAINS + v, n)

    def layer_mate(offset):
        dy, dx, dc = offset
        y_to = (y + dy) % 4
        v_to = (y_to // 2) * 2 + (core + dc) % 2
        n_to = (y_to % 2) * 4 + (x + dx) % 4
        return v_to, n_to, (place * DOMAINS + v_to, n_to)

    ring = [o[0] for o in far_first((RING,))]
    layer = far_first((4, 4, 2))

    barrier = pltpu.get_barrier_semaphore()
    for offset in ring:
        pl.semaphore_signal(barrier, inc=1, device_id=ring_mate(offset)[1], device_id_type=MESH)
    for offset in layer:
        pl.semaphore_signal(barrier, inc=1, device_id=layer_mate(offset)[2], device_id_type=MESH)

    inputs = (
        (count_hbm, count_ref),
        (factor_hbm, factor_ref),
        (offset_hbm, offset_ref),
        (base_hbm, base_ref),
        (charge_hbm, charge_ref),
        (zh_hbm, zh_ref),
        (zl_hbm, zl_ref),
        (yth_hbm, yth_ref),
        (ytl_hbm, ytl_ref),
        (zfactor_hbm, zfactor_ref),
        (gain_hbm, gain_ref),
        (square_hbm, square_ref),
        (xh_hbm, xh_ref),
        (xl_hbm, xl_ref),
        (xth_hbm, xth_ref),
        (xtl_hbm, xtl_ref),
        (yh_hbm, yh_ref),
        (yl_hbm, yl_ref),
    )
    loads = [pltpu.make_async_copy(a, b, local_sems.at[i]) for i, (a, b) in enumerate(inputs)]
    for load in loads:
        load.start()

    lanes = lax.broadcasted_iota(jnp.int32, (1, 128), 1)
    low_lanes = lanes < HALF
    low_rows = lax.broadcasted_iota(jnp.int32, (1, 8, 1), 1) < CX

    for load in loads[:5]:
        load.wait()
    t = [offset_ref[d, 0] for d in range(3)]
    corner = [base_ref[d, 0] for d in range(3)]
    weights = [spline_weights(u) for u in t]
    slopes = [spline_slopes(u) for u in t]
    occupied = lax.broadcasted_iota(jnp.int32, (1, SLOTS), 1) < count_ref[...]
    charge = jnp.where(occupied, charge_ref[0], 0.0)

    def depth_steps(first):
        cell = lax.broadcasted_iota(jnp.int32, (128, SLOTS), 0) + first
        return (cell - corner[2]) & (NZ - 1)

    for first in range(0, NZ, 128):
        high, low = split(pick(depth_steps(first), weights[2]))
        depth_h[first : first + 128, :] = high
        depth_l[first : first + 128, :] = low

    row_steps = lax.broadcasted_iota(jnp.int32, (16, SLOTS), 0) - corner[1]
    row_q = pick(row_steps, weights[1]) * charge
    plane_w = [pick(p - corner[0], weights[0]) for p in range(PLANES)]
    cross = jnp.concatenate([row_q * plane_w[p] for p in range(PLANES)], axis=0)
    grid = dot3(split(cross), (depth_h[...], depth_l[...]), ((1,), (1,)))
    for load in loads[5:7]:
        load.wait()
    spectrum = dot3(split(grid), (zh_ref[...], zl_ref[...]), ((1,), (0,)))
    for m in range(DOMAINS):
        tiles = [spectrum[16 * p : 16 * p + 16, 128 * m : 128 * m + 128] for p in range(PLANES)]
        tiles = exchange_lanes(tiles + [jnp.zeros((16, 128), F32)], lanes)
        for e in range(NARROW):
            send_a[16 * (8 * m + e) : 16 * (8 * m + e) + 16, :] = tiles[e]

    pl.semaphore_wait(barrier, len(ring) + len(layer))

    def push(stage, source, target, to):
        pltpu.make_async_remote_copy(
            src_ref=source,
            dst_ref=target,
            send_sem=send_sems.at[stage],
            recv_sem=recv_sems.at[stage],
            device_id=to,
            device_id_type=MESH,
        ).start()

    def drain(stage, block):
        return pltpu.make_async_remote_copy(
            src_ref=block,
            dst_ref=block,
            send_sem=send_sems.at[stage],
            recv_sem=recv_sems.at[stage],
            device_id=(w, n),
            device_id_type=MESH,
        )

    mine = 8 * v + n
    own_a = recv_a.at[pl.ds(ROWS * mine, ROWS)]
    for offset in layer:
        v_to, n_to, to = layer_mate(offset)
        push(0, send_a.at[pl.ds(16 * (8 * v_to + n_to), ROWS)], own_a, to)
    keep_a = pltpu.make_async_copy(send_a.at[pl.ds(16 * mine, ROWS)], own_a, local_sems.at[18])
    keep_a.start()

    for first in range(0, NZ, 128):
        high, low = split(pick(depth_steps(first), slopes[2]))
        slope_h[first : first + 128, :] = high
        slope_l[first : first + 128, :] = low
    for load in loads[7:]:
        load.wait()
    coefficient = 128 * v + 8 * place + n
    chosen = lax.broadcasted_iota(jnp.int32, (8, NZ), 1) == coefficient
    zfactor = jnp.sum(jnp.where(chosen, zfactor_ref[...], 0.0), axis=1, keepdims=True)
    squared = square_ref[...] + zfactor[0:1]
    positive = jnp.where(squared > 0.0, squared, 1.0)
    influence = jnp.where(squared > 0.0, gain_ref[...] * zfactor[1:2] / positive, 0.0)

    keep_a.wait()
    drain(0, recv_a.at[pl.ds(0, ROWS * 31)]).wait_recv()
    half = 8 * ROWS * 2
    rows = jnp.concatenate([recv_a[:half], recv_a[half:]], axis=1)
    columns = dot3((yth_ref[...], ytl_ref[...]), split(rows), ((1,), (0,)))
    first = columns[:, :128].T.reshape(RING, 8, 128)
    second = columns[:, 128:].T.reshape(RING, 8, 128)

    def both(value):
        return swap(value.reshape(8 * RING, 128)).reshape(RING, 8, 128)

    def turn(value):
        return pltpu.roll(value, CX, 1)

    first_swapped = both(first)
    second_swapped = both(second)
    low3 = low_lanes.reshape(1, 1, 128)
    upper = first + jnp.where(low3, 0.0, turn(first_swapped))
    lower = turn(second) + jnp.where(low3, first_swapped, second_swapped)
    send_b[:, 0:8, :] = jnp.where(low_rows, upper, lower)
    send_b[:, 8:16, :] = turn(second_swapped)

    for offset in ring:
        other, to = ring_mate(offset)
        push(1, send_b.at[other, pl.ds(0, 12)], recv_b.at[place, pl.ds(0, 12)], to)
    recv_b[place] = send_b[place]
    drain(1, recv_b.at[pl.ds(0, 15), pl.ds(0, 12)]).wait_recv()

    beyond = recv_b[:, 8:16, :]
    beyond = jnp.concatenate([beyond[RING - 1 :], beyond[: RING - 1]], axis=0)
    planes = recv_b[:, 0:8, :] + jnp.where(low_rows & low3, beyond, 0.0)
    planes = planes.reshape(8 * RING, 128)
    turned = swap(planes)
    stacked = jnp.concatenate(
        [jnp.where(low_lanes, planes, turned), jnp.where(low_lanes, turned, planes)], axis=0
    )
    filtered = dot3((xh_ref[...], xl_ref[...]), split(stacked), ((1,), (0,))) * influence
    planes = dot3((xth_ref[...], xtl_ref[...]), split(filtered), ((1,), (0,)))
    planes = jnp.where(low_lanes, planes[:128], planes[128:]).reshape(RING, 8, 128)
    send_c[:, 0:8, :] = planes
    send_c[:, 8:16, :] = jnp.concatenate([planes[1:], planes[:1]], axis=0)

    for offset in ring:
        other, to = ring_mate(offset)
        push(2, send_c.at[other, pl.ds(0, 12)], recv_c.at[place, pl.ds(0, 12)], to)
    recv_c[place] = send_c[place]
    drain(2, recv_c.at[pl.ds(0, 15), pl.ds(0, 12)]).wait_recv()

    own = recv_c[:, 0:8, :]
    own_swapped = both(own)
    beyond = turn(both(recv_c[:, 8:16, :]))
    first = jnp.where(low_rows, own, jnp.where(low3, turn(own_swapped), own_swapped))
    second = jnp.where(low_rows, turn(own), jnp.where(low3, own_swapped, beyond))
    columns = jnp.concatenate([first, second], axis=0).reshape(16 * RING, 128)
    rows = dot3((yh_ref[...], yl_ref[...]), split(columns), ((1,), (1,)))
    send_d[0] = rows[:, :128]
    send_d[1] = rows[:, 128:]

    own_d = recv_d.at[pl.ds(16 * mine, ROWS)]

    def block_d(v_to, n_to):
        return send_d.at[v_to // 2, pl.ds(ROWS * (8 * (v_to % 2) + n_to), ROWS)]

    for offset in layer:
        v_to, n_to, to = layer_mate(offset)
        push(3, block_d(v_to, n_to), own_d, to)
    keep_d = pltpu.make_async_copy(block_d(v, n), own_d, local_sems.at[19])
    keep_d.start()
    keep_d.wait()
    drain(3, recv_a.at[pl.ds(0, ROWS * 31)]).wait_recv()

    inside = lax.broadcasted_iota(jnp.int32, (16, 128), 0) < ROWS
    parts = []
    for m in range(DOMAINS):
        tiles = [recv_d[16 * (8 * m + e) : 16 * (8 * m + e) + 16, :] for e in range(NARROW)]
        tiles = exchange_lanes([jnp.where(inside, u, 0.0) for u in tiles], lanes)
        parts.append(jnp.concatenate(tiles[:PLANES], axis=0))
    spectrum = jnp.concatenate(parts, axis=1)
    potential = split(dot3(split(spectrum), (zh_ref[...], zl_ref[...]), ((1,), (1,))))
    along_w = dot3(potential, (depth_h[...], depth_l[...]), ((1,), (0,)))
    along_s = dot3(potential, (slope_h[...], slope_l[...]), ((1,), (0,)))

    total = jnp.zeros((16, SLOTS), F32)
    pull_x, pull_z = total, total
    for p in range(PLANES):
        part = slice(16 * p, 16 * p + 16)
        total = total + along_w[part] * plane_w[p]
        pull_x = pull_x + along_w[part] * pick(p - corner[0], slopes[0])
        pull_z = pull_z + along_s[part] * plane_w[p]

    def over_rows(value):
        return jnp.sum(value, axis=0, keepdims=True)

    factor = factor_ref[...]
    row_w = pick(row_steps, weights[1])
    pull_y = over_rows(total * pick(row_steps, slopes[1]))
    total = over_rows(total * row_w)
    pull_x = over_rows(pull_x * row_w)
    pull_z = over_rows(pull_z * row_w)
    grad_ref[0] = jnp.where(occupied, factor * total, 0.0)
    pull = -factor * charge
    force_ref[0, 0] = pull * pull_x
    force_ref[1, 0] = pull * pull_y
    force_ref[2, 0] = pull * pull_z

    drain(0, recv_a.at[pl.ds(0, ROWS * 31)]).wait_send()
    drain(1, recv_b.at[pl.ds(0, 15), pl.ds(0, 12)]).wait_send()
    drain(2, recv_c.at[pl.ds(0, 15), pl.ds(0, 12)]).wait_send()
    drain(3, recv_a.at[pl.ds(0, ROWS * 31)]).wait_send()


def on_device(offsets, bases, charges, counts, cotangent):
    z_pair = halves(real_basis(NZ)[0].T)
    y_table = row_matrix()
    x_table = real_basis(NX)[0][:, plane_order()]
    square_x, gain_x = frequency_factors(NX)
    square_y, gain_y = frequency_factors(NY)
    zfactor = np.zeros((8, NZ), np.float32)
    zfactor[0], zfactor[1] = frequency_factors(NZ)
    square = (square_x[:, None] + np.tile(square_y, 2)[None, :]).astype(np.float32)
    gain = (gain_x[:, None] * np.tile(gain_y, 2)[None, :] / math.pi).astype(np.float32)
    arrays = (
        counts,
        cotangent,
        offsets,
        bases,
        charges,
        *z_pair,
        *halves(y_table),
        *halves(y_table.T),
        *halves(x_table),
        *halves(x_table.T),
        gain,
        square,
        zfactor,
    )
    hbm = pl.BlockSpec(memory_space=pltpu.HBM)
    vmem = pl.BlockSpec(memory_space=VMEM)
    return pl.pallas_call(
        kernel,
        out_shape=(
            jax.ShapeDtypeStruct((3, 1, 1, SLOTS), F32),
            jax.ShapeDtypeStruct((1, 1, SLOTS), F32),
        ),
        in_specs=[hbm] * len(arrays),
        out_specs=(vmem, vmem),
        scratch_shapes=[
            *[VMEM(a.shape, a.dtype) for a in arrays],
            VMEM((16 * 32, 128), F32),
            VMEM((ROWS * 32, 128), F32),
            VMEM((RING, 16, 128), F32),
            VMEM((RING, 16, 128), F32),
            VMEM((RING, 16, 128), F32),
            VMEM((RING, 16, 128), F32),
            VMEM((2, ROWS * 16, 128), F32),
            VMEM((16 * 32, 128), F32),
            VMEM((NZ, SLOTS), BF16),
            VMEM((NZ, SLOTS), BF16),
            VMEM((NZ, SLOTS), BF16),
            VMEM((NZ, SLOTS), BF16),
            pltpu.SemaphoreType.DMA((4,)),
            pltpu.SemaphoreType.DMA((4,)),
            pltpu.SemaphoreType.DMA((len(arrays) + 2,)),
        ],
        compiler_params=pltpu.CompilerParams(
            collective_id=0, has_side_effects=True, vmem_limit_bytes=63 * 1024 * 1024
        ),
        name="ewald",
    )(*arrays)


def solution(mesh):
    placed = (
        P(None, "wide", "narrow", None),
        P(None, "wide", "narrow", None),
        P("wide", "narrow", None),
        P("wide", "narrow"),
        P(),
    )
    return jax.shard_map(
        on_device,
        mesh=mesh,
        in_specs=placed,
        out_specs=(P(None, "wide", "narrow", None), P("wide", "narrow", None)),
        check_vma=False,
    )
```

```python
import math

import jax
import jax.numpy as jnp
import ml_dtypes
import numpy as np
from jax import lax
from jax.experimental import pallas as pl
from jax.experimental.pallas import tpu as pltpu
from jax.sharding import PartitionSpec as P

CX = 4
CY = 8
NZ = 512
WIDE = 64
NARROW = 8
NX = CX * WIDE
NY = CY * NARROW
SLOTS = 512
ROWS = CY + 3
RING = 16
DOMAINS = WIDE // RING
PLANES = CX + 3
REACH = RING // 4
HALF = 64
MESH = pl.DeviceIdType.MESH
VMEM = pltpu.VMEM
F32 = jnp.float32
BF16 = jnp.bfloat16


def real_basis(length):
    c = np.arange(length)
    freq = np.where(c <= length // 2, c, length - c)
    phase = (freq[:, None] * c[None, :]) % length * (2.0 * np.pi / length)
    scale = np.where((freq == 0) | (2 * freq == length), 1.0, np.sqrt(2.0)) / np.sqrt(length)
    table = np.where((c <= length // 2)[:, None], np.cos(phase), np.sin(phase)) * scale[:, None]
    return table, freq


def halves(table):
    table = np.asarray(table, np.float32)
    high = table.astype(ml_dtypes.bfloat16)
    low = (table - high.astype(np.float32)).astype(ml_dtypes.bfloat16)
    return high, low


def frequency_factors(length):
    freq = real_basis(length)[1]
    square = (freq / length) ** 2
    spline = 9.0 / (2.0 + np.cos(2.0 * np.pi * freq / length)) ** 2
    return square, np.exp(-(np.pi**2) * square) * spline


def row_matrix():
    basis = real_basis(NY)[0]
    table = np.zeros((2, NARROW, ROWS, 2, NY))
    for half in range(2):
        for n in range(NARROW):
            for r in range(ROWS):
                table[half, n, r, half] = basis[:, (CY * n + r) % NY]
    return table.reshape(2 * NARROW * ROWS, 2 * NY)


def plane_order():
    half, place, other, plane = np.meshgrid(
        np.arange(2), np.arange(RING), np.arange(2), np.arange(CX), indexing="ij"
    )
    return (CX * (DOMAINS * place + 2 * other + half) + plane).reshape(-1)


def split(value):
    high = value.astype(BF16)
    return high, (value - high.astype(F32)).astype(BF16)


def dot3(a, b, contract):
    dims = (contract, ((), ()))

    def one(x, y):
        return lax.dot_general(x, y, dims, preferred_element_type=F32)

    return one(a[0], b[0]) + (one(a[0], b[1]) + one(a[1], b[0]))


def pick(steps, values):
    out = jnp.where(steps == 3, values[3], 0.0)
    for j in (2, 1, 0):
        out = jnp.where(steps == j, values[j], out)
    return out


def spline_weights(t):
    s = 1.0 - t
    square = t * t
    cube = square * t
    return (
        s * s * s / 6.0,
        (3.0 * cube - 6.0 * square + 4.0) / 6.0,
        (-3.0 * cube + 3.0 * square + 3.0 * t + 1.0) / 6.0,
        cube / 6.0,
    )


def spline_slopes(t):
    s = 1.0 - t
    square = t * t
    return (-0.5 * s * s, 1.5 * square - 2.0 * t, -1.5 * square + t + 0.5, 0.5 * square)


def swap(value):
    return pltpu.roll(value, HALF, 1)


def exchange_lanes(blocks, lanes):
    blocks = list(blocks)
    for bit in range(3):
        step = 1 << bit
        clear = (lanes & step) == 0
        for a in range(8):
            if not a & step:
                x, y = blocks[a], blocks[a + step]
                blocks[a] = jnp.where(clear, x, pltpu.roll(y, step, 1))
                blocks[a + step] = jnp.where(clear, pltpu.roll(x, 128 - step, 1), y)
    return blocks


def far_first(sizes):
    offsets = [o for o in np.ndindex(*sizes) if any(o)]

    def hops(offset):
        return sum(min(o, size - o) for o, size in zip(offset, sizes))

    return sorted(offsets, key=lambda o: -hops(o))


def kernel(
    count_hbm,
    factor_hbm,
    offset_hbm,
    base_hbm,
    charge_hbm,
    zh_hbm,
    zl_hbm,
    zth_hbm,
    ztl_hbm,
    yh_hbm,
    yl_hbm,
    yth_hbm,
    ytl_hbm,
    xh_hbm,
    xl_hbm,
    xth_hbm,
    xtl_hbm,
    gain_hbm,
    square_hbm,
    zfactor_hbm,
    raw_ref,
    count_ref,
    factor_ref,
    offset_ref,
    base_ref,
    charge_ref,
    zh_ref,
    zl_ref,
    zth_ref,
    ztl_ref,
    yh_ref,
    yl_ref,
    yth_ref,
    ytl_ref,
    xh_ref,
    xl_ref,
    xth_ref,
    xtl_ref,
    gain_ref,
    square_ref,
    zfactor_ref,
    send_a,
    recv_a,
    send_b,
    recv_b,
    send_c,
    recv_c,
    send_d,
    recv_d,
    depth_h,
    depth_l,
    atom_h,
    atom_l,
    send_sems,
    recv_sems,
    local_sems,
    ring_sem,
):
    w = lax.axis_index("wide")
    n = lax.axis_index("narrow")
    place = w // DOMAINS
    v = w % DOMAINS
    core = v % 2
    y = (v // 2) * 2 + n // 4
    x = n % 4

    def ring_mate(offset):
        other = (place + offset) % RING
        return other, (other * DOMAINS + v, n)

    def layer_mate(offset):
        dy, dx, dc = offset
        y_to = (y + dy) % 4
        v_to = (y_to // 2) * 2 + (core + dc) % 2
        n_to = (y_to % 2) * 4 + (x + dx) % 4
        return v_to, n_to, (place * DOMAINS + v_to, n_to)

    ring = [o[0] for o in far_first((RING,))]
    layer = far_first((4, 4, 2))

    barrier = pltpu.get_barrier_semaphore()
    near = [o for o in ring if min(o, RING - o) <= REACH]
    for offset in near:
        pl.semaphore_signal(barrier, inc=1, device_id=ring_mate(offset)[1], device_id_type=MESH)
    for offset in layer:
        pl.semaphore_signal(barrier, inc=1, device_id=layer_mate(offset)[2], device_id_type=MESH)

    inputs = (
        (count_hbm, count_ref),
        (factor_hbm, factor_ref),
        (offset_hbm, offset_ref),
        (base_hbm, base_ref),
        (charge_hbm, charge_ref),
        (zh_hbm, zh_ref),
        (zl_hbm, zl_ref),
        (yth_hbm, yth_ref),
        (ytl_hbm, ytl_ref),
        (zfactor_hbm, zfactor_ref),
        (gain_hbm, gain_ref),
        (square_hbm, square_ref),
        (xh_hbm, xh_ref),
        (xl_hbm, xl_ref),
        (xth_hbm, xth_ref),
        (xtl_hbm, xtl_ref),
        (yh_hbm, yh_ref),
        (yl_hbm, yl_ref),
        (zth_hbm, zth_ref),
        (ztl_hbm, ztl_ref),
    )
    loads = [pltpu.make_async_copy(a, b, local_sems.at[i]) for i, (a, b) in enumerate(inputs)]
    for load in loads:
        load.start()

    lanes = lax.broadcasted_iota(jnp.int32, (1, 128), 1)
    low_lanes = lanes < HALF
    low_rows = lax.broadcasted_iota(jnp.int32, (1, 8, 1), 1) < CX

    for load in loads[:5]:
        load.wait()
    t = [offset_ref[d, 0] for d in range(3)]
    corner = [base_ref[d, 0] for d in range(3)]
    weights = [spline_weights(u) for u in t]
    slopes = [spline_slopes(u) for u in t]
    occupied = lax.broadcasted_iota(jnp.int32, (1, SLOTS), 1) < count_ref[...]
    charge = jnp.where(occupied, charge_ref[0], 0.0)

    def depth_steps(first):
        cell = lax.broadcasted_iota(jnp.int32, (128, SLOTS), 0) + first
        return (cell - corner[2]) & (NZ - 1)

    for first in range(0, NZ, 128):
        high, low = split(pick(depth_steps(first), weights[2]))
        depth_h[first : first + 128, :SLOTS] = high
        depth_l[first : first + 128, :SLOTS] = low

    row_steps = lax.broadcasted_iota(jnp.int32, (16, SLOTS), 0) - corner[1]
    row_w = pick(row_steps, weights[1])
    row_q = row_w * charge
    plane_w = [pick(p - corner[0], weights[0]) for p in range(PLANES)]
    cross = jnp.concatenate([row_q * plane_w[p] for p in range(PLANES)], axis=0)
    grid = dot3(split(cross), (depth_h[:, :SLOTS], depth_l[:, :SLOTS]), ((1,), (1,)))
    for load in loads[5:7]:
        load.wait()
    spectrum = dot3(split(grid), (zh_ref[...], zl_ref[...]), ((1,), (0,)))
    for m in range(DOMAINS):
        tiles = [spectrum[16 * p : 16 * p + 16, 128 * m : 128 * m + 128] for p in range(PLANES)]
        tiles = exchange_lanes(tiles + [jnp.zeros((16, 128), F32)], lanes)
        for e in range(NARROW):
            send_a[16 * (8 * m + e) : 16 * (8 * m + e) + 16, :] = tiles[e]

    pl.semaphore_wait(barrier, len(near) + len(layer))

    def push(stage, source, target, to):
        pltpu.make_async_remote_copy(
            src_ref=source,
            dst_ref=target,
            send_sem=send_sems.at[stage],
            recv_sem=recv_sems.at[stage],
            device_id=to,
            device_id_type=MESH,
        ).start()

    def drain(stage, block):
        return pltpu.make_async_remote_copy(
            src_ref=block,
            dst_ref=block,
            send_sem=send_sems.at[stage],
            recv_sem=recv_sems.at[stage],
            device_id=(w, n),
            device_id_type=MESH,
        )

    mine = 8 * v + n
    own_a = recv_a.at[pl.ds(ROWS * mine, ROWS)]
    for offset in layer:
        v_to, n_to, to = layer_mate(offset)
        push(0, send_a.at[pl.ds(16 * (8 * v_to + n_to), ROWS)], own_a, to)
    keep_a = pltpu.make_async_copy(send_a.at[pl.ds(16 * mine, ROWS)], own_a, local_sems.at[20])
    keep_a.start()
    for offset in (REACH, RING - REACH):
        pl.semaphore_signal(ring_sem, inc=1, device_id=ring_mate(offset)[1], device_id_type=MESH)

    row_s = pick(row_steps, slopes[1])
    plane_s = [pick(p - corner[0], slopes[0]) for p in range(PLANES)]
    for first in range(0, NZ, 128):
        high, low = split(pick(depth_steps(first), slopes[2]))
        depth_h[first : first + 128, SLOTS:] = high
        depth_l[first : first + 128, SLOTS:] = low
    for load in loads[7:]:
        load.wait()
    coefficient = 128 * v + 8 * place + n
    chosen = lax.broadcasted_iota(jnp.int32, (8, NZ), 1) == coefficient
    zfactor = jnp.sum(jnp.where(chosen, zfactor_ref[...], 0.0), axis=1, keepdims=True)
    squared = square_ref[...] + zfactor[0:1]
    positive = jnp.where(squared > 0.0, squared, 1.0)
    influence = jnp.where(squared > 0.0, gain_ref[...] * zfactor[1:2] / positive, 0.0)

    keep_a.wait()
    drain(0, recv_a.at[pl.ds(0, ROWS * 31)]).wait_recv()
    half = 8 * ROWS * 2
    rows = jnp.concatenate([recv_a[:half], recv_a[half:]], axis=1)
    columns = dot3((yth_ref[...], ytl_ref[...]), split(rows), ((1,), (0,)))
    first = columns[:, :128].T.reshape(RING, 8, 128)
    second = columns[:, 128:].T.reshape(RING, 8, 128)

    def both(value):
        return swap(value.reshape(8 * RING, 128)).reshape(RING, 8, 128)

    def turn(value):
        return pltpu.roll(value, CX, 1)

    first_swapped = both(first)
    second_swapped = both(second)
    low3 = low_lanes.reshape(1, 1, 128)
    upper = first + jnp.where(low3, 0.0, turn(first_swapped))
    lower = turn(second) + jnp.where(low3, first_swapped, second_swapped)
    send_b[:, 0:8, :] = jnp.where(low_rows, upper, lower)
    send_b[:, 8:16, :] = turn(second_swapped)

    pl.semaphore_wait(ring_sem, 2)
    for offset in ring:
        other, to = ring_mate(offset)
        push(1, send_b.at[other, pl.ds(0, 12)], recv_b.at[place, pl.ds(0, 12)], to)
    recv_b[place] = send_b[place]
    for first in range(0, NZ, 128):
        part = slice(first, first + 128)
        z_rows = (zth_ref[part, :], ztl_ref[part, :])
        high, low = split(dot3(z_rows, (depth_h[...], depth_l[...]), ((1,), (0,))))
        atom_h[part, :] = high
        atom_l[part, :] = low
    drain(1, recv_b.at[pl.ds(0, 15), pl.ds(0, 12)]).wait_recv()

    beyond = recv_b[:, 8:16, :]
    beyond = jnp.concatenate([beyond[RING - 1 :], beyond[: RING - 1]], axis=0)
    planes = recv_b[:, 0:8, :] + jnp.where(low_rows & low3, beyond, 0.0)
    planes = planes.reshape(8 * RING, 128)
    turned = swap(planes)
    stacked = jnp.concatenate(
        [jnp.where(low_lanes, planes, turned), jnp.where(low_lanes, turned, planes)], axis=0
    )
    filtered = dot3((xh_ref[...], xl_ref[...]), split(stacked), ((1,), (0,))) * influence
    planes = dot3((xth_ref[...], xtl_ref[...]), split(filtered), ((1,), (0,)))
    planes = jnp.where(low_lanes, planes[:128], planes[128:]).reshape(RING, 8, 128)
    send_c[:, 0:8, :] = planes
    send_c[:, 8:16, :] = jnp.concatenate([planes[1:], planes[:1]], axis=0)

    for offset in ring:
        other, to = ring_mate(offset)
        push(2, send_c.at[other, pl.ds(0, 12)], recv_c.at[place, pl.ds(0, 12)], to)
    recv_c[place] = send_c[place]
    drain(2, recv_c.at[pl.ds(0, 15), pl.ds(0, 12)]).wait_recv()

    own = recv_c[:, 0:8, :]
    own_swapped = both(own)
    beyond = turn(both(recv_c[:, 8:16, :]))
    first = jnp.where(low_rows, own, jnp.where(low3, turn(own_swapped), own_swapped))
    second = jnp.where(low_rows, turn(own), jnp.where(low3, own_swapped, beyond))
    columns = jnp.concatenate([first, second], axis=0).reshape(16 * RING, 128)
    rows = dot3((yh_ref[...], yl_ref[...]), split(columns), ((1,), (1,)))
    send_d[0] = rows[:, :128]
    send_d[1] = rows[:, 128:]

    own_d = recv_d.at[pl.ds(16 * mine, ROWS)]

    def block_d(v_to, n_to):
        return send_d.at[v_to // 2, pl.ds(ROWS * (8 * (v_to % 2) + n_to), ROWS)]

    for offset in layer:
        v_to, n_to, to = layer_mate(offset)
        push(3, block_d(v_to, n_to), own_d, to)
    keep_d = pltpu.make_async_copy(block_d(v, n), own_d, local_sems.at[21])
    keep_d.start()
    keep_d.wait()
    drain(3, recv_a.at[pl.ds(0, ROWS * 31)]).wait_recv()

    inside = lax.broadcasted_iota(jnp.int32, (16, 128), 0) < ROWS
    parts = []
    for m in range(DOMAINS):
        tiles = [recv_d[16 * (8 * m + e) : 16 * (8 * m + e) + 16, :] for e in range(NARROW)]
        tiles = exchange_lanes([jnp.where(inside, u, 0.0) for u in tiles], lanes)
        parts.append(jnp.concatenate(tiles[:PLANES], axis=0))
    spectrum = jnp.concatenate(parts, axis=1)
    along = dot3(split(spectrum), (atom_h[...], atom_l[...]), ((1,), (0,)))

    total = jnp.zeros((16, SLOTS), F32)
    pull_x, pull_z = total, total
    for p in range(PLANES):
        part = slice(16 * p, 16 * p + 16)
        total = total + along[part, :SLOTS] * plane_w[p]
        pull_x = pull_x + along[part, :SLOTS] * plane_s[p]
        pull_z = pull_z + along[part, SLOTS:] * plane_w[p]

    def over_rows(value):
        return jnp.sum(value, axis=0, keepdims=True)

    factor = factor_ref[...]
    pull_y = over_rows(total * row_s)
    total = over_rows(total * row_w)
    pull_x = over_rows(pull_x * row_w)
    pull_z = over_rows(pull_z * row_w)
    pull = -factor * charge
    raw_ref[0, 0] = pull * pull_x
    raw_ref[1, 0] = pull * pull_y
    raw_ref[2, 0] = pull * pull_z
    raw_ref[3, 0] = jnp.where(occupied, factor * total, 0.0)

    drain(0, recv_a.at[pl.ds(0, ROWS * 31)]).wait_send()
    drain(1, recv_b.at[pl.ds(0, 15), pl.ds(0, 12)]).wait_send()
    drain(2, recv_c.at[pl.ds(0, 15), pl.ds(0, 12)]).wait_send()
    drain(3, recv_a.at[pl.ds(0, ROWS * 31)]).wait_send()


def hand_out(raw_ref, force_ref, grad_ref):
    force_ref[...] = raw_ref[0:3]
    grad_ref[...] = raw_ref[3]


def on_device(offsets, bases, charges, counts, cotangent):
    z_table = real_basis(NZ)[0].T
    y_table = row_matrix()
    x_table = real_basis(NX)[0][:, plane_order()]
    square_x, gain_x = frequency_factors(NX)
    square_y, gain_y = frequency_factors(NY)
    zfactor = np.zeros((8, NZ), np.float32)
    zfactor[0], zfactor[1] = frequency_factors(NZ)
    square = (square_x[:, None] + np.tile(square_y, 2)[None, :]).astype(np.float32)
    gain = (gain_x[:, None] * np.tile(gain_y, 2)[None, :] / math.pi).astype(np.float32)
    arrays = (
        counts,
        cotangent,
        offsets,
        bases,
        charges,
        *halves(z_table),
        *halves(z_table.T),
        *halves(y_table),
        *halves(y_table.T),
        *halves(x_table),
        *halves(x_table.T),
        gain,
        square,
        zfactor,
    )
    hbm = pl.BlockSpec(memory_space=pltpu.HBM)
    vmem = pl.BlockSpec(memory_space=VMEM)
    raw = pl.pallas_call(
        kernel,
        out_shape=jax.ShapeDtypeStruct((4, 1, 1, SLOTS), F32),
        in_specs=[hbm] * len(arrays),
        out_specs=vmem,
        scratch_shapes=[
            *[VMEM(a.shape, a.dtype) for a in arrays],
            VMEM((16 * 32, 128), F32),
            VMEM((ROWS * 32, 128), F32),
            VMEM((RING, 16, 128), F32),
            VMEM((RING, 16, 128), F32),
            VMEM((RING, 16, 128), F32),
            VMEM((RING, 16, 128), F32),
            VMEM((2, ROWS * 16, 128), F32),
            VMEM((16 * 32, 128), F32),
            VMEM((NZ, 2 * SLOTS), BF16),
            VMEM((NZ, 2 * SLOTS), BF16),
            VMEM((NZ, 2 * SLOTS), BF16),
            VMEM((NZ, 2 * SLOTS), BF16),
            pltpu.SemaphoreType.DMA((4,)),
            pltpu.SemaphoreType.DMA((4,)),
            pltpu.SemaphoreType.DMA((len(arrays) + 2,)),
            pltpu.SemaphoreType.REGULAR,
        ],
        compiler_params=pltpu.CompilerParams(
            collective_id=0, has_side_effects=True, vmem_limit_bytes=63 * 1024 * 1024
        ),
        name="ewald",
    )(*arrays)
    return pl.pallas_call(
        hand_out,
        out_shape=(
            jax.ShapeDtypeStruct((3, 1, 1, SLOTS), F32),
            jax.ShapeDtypeStruct((1, 1, SLOTS), F32),
        ),
        in_specs=[vmem],
        out_specs=(vmem, vmem),
        name="hand_out",
    )(raw)


def solution(mesh):
    placed = (
        P(None, "wide", "narrow", None),
        P(None, "wide", "narrow", None),
        P("wide", "narrow", None),
        P("wide", "narrow"),
        P(),
    )
    return jax.shard_map(
        on_device,
        mesh=mesh,
        in_specs=placed,
        out_specs=(P(None, "wide", "narrow", None), P("wide", "narrow", None)),
        check_vma=False,
    )
```

```python
import math

import jax
import jax.numpy as jnp
import ml_dtypes
import numpy as np
from jax import lax
from jax.experimental import pallas as pl
from jax.experimental.pallas import tpu as pltpu
from jax.sharding import PartitionSpec as P

CX = 4
CY = 8
NZ = 512
WIDE = 64
NARROW = 8
NX = CX * WIDE
NY = CY * NARROW
SLOTS = 512
ROWS = CY + 3
RING = 16
DOMAINS = WIDE // RING
PLANES = CX + 3
REACH = RING // 4
HALF = 64
MESH = pl.DeviceIdType.MESH
VMEM = pltpu.VMEM
F32 = jnp.float32
BF16 = jnp.bfloat16


def real_basis(length):
    c = np.arange(length)
    freq = np.where(c <= length // 2, c, length - c)
    phase = (freq[:, None] * c[None, :]) % length * (2.0 * np.pi / length)
    scale = np.where((freq == 0) | (2 * freq == length), 1.0, np.sqrt(2.0)) / np.sqrt(length)
    table = np.where((c <= length // 2)[:, None], np.cos(phase), np.sin(phase)) * scale[:, None]
    return table, freq


def halves(table):
    table = np.asarray(table, np.float32)
    high = table.astype(ml_dtypes.bfloat16)
    low = (table - high.astype(np.float32)).astype(ml_dtypes.bfloat16)
    return high, low


def frequency_factors(length):
    freq = real_basis(length)[1]
    square = (freq / length) ** 2
    spline = 9.0 / (2.0 + np.cos(2.0 * np.pi * freq / length)) ** 2
    return square, np.exp(-(np.pi**2) * square) * spline


def row_matrix():
    basis = real_basis(NY)[0]
    table = np.zeros((2, NARROW, ROWS, 2, NY))
    for half in range(2):
        for n in range(NARROW):
            for r in range(ROWS):
                table[half, n, r, half] = basis[:, (CY * n + r) % NY]
    return table.reshape(2 * NARROW * ROWS, 2 * NY)


def plane_order():
    half, place, other, plane = np.meshgrid(
        np.arange(2), np.arange(RING), np.arange(2), np.arange(CX), indexing="ij"
    )
    return (CX * (DOMAINS * place + 2 * other + half) + plane).reshape(-1)


def split(value):
    high = value.astype(BF16)
    return high, (value - high.astype(F32)).astype(BF16)


def dot3(a, b, contract):
    dims = (contract, ((), ()))

    def one(x, y):
        return lax.dot_general(x, y, dims, preferred_element_type=F32)

    return one(a[0], b[0]) + (one(a[0], b[1]) + one(a[1], b[0]))


def pick(steps, values):
    out = jnp.where(steps == 3, values[3], 0.0)
    for j in (2, 1, 0):
        out = jnp.where(steps == j, values[j], out)
    return out


def spline_weights(t):
    s = 1.0 - t
    square = t * t
    cube = square * t
    return (
        s * s * s / 6.0,
        (3.0 * cube - 6.0 * square + 4.0) / 6.0,
        (-3.0 * cube + 3.0 * square + 3.0 * t + 1.0) / 6.0,
        cube / 6.0,
    )


def spline_slopes(t):
    s = 1.0 - t
    square = t * t
    return (-0.5 * s * s, 1.5 * square - 2.0 * t, -1.5 * square + t + 0.5, 0.5 * square)


def swap(value):
    return pltpu.roll(value, HALF, 1)


def exchange_lanes(blocks, lanes):
    blocks = list(blocks)
    for bit in range(3):
        step = 1 << bit
        clear = (lanes & step) == 0
        for a in range(8):
            if not a & step:
                x, y = blocks[a], blocks[a + step]
                blocks[a] = jnp.where(clear, x, pltpu.roll(y, step, 1))
                blocks[a + step] = jnp.where(clear, pltpu.roll(x, 128 - step, 1), y)
    return blocks


def far_first(sizes):
    offsets = [o for o in np.ndindex(*sizes) if any(o)]

    def hops(offset):
        return sum(min(o, size - o) for o, size in zip(offset, sizes))

    return sorted(offsets, key=lambda o: -hops(o))


def kernel(
    count_ref,
    factor_ref,
    offset_hbm,
    base_hbm,
    charge_hbm,
    zh_hbm,
    zl_hbm,
    zth_hbm,
    ztl_hbm,
    yh_hbm,
    yl_hbm,
    yth_hbm,
    ytl_hbm,
    xh_hbm,
    xl_hbm,
    xth_hbm,
    xtl_hbm,
    gain_hbm,
    square_hbm,
    zfactor_hbm,
    raw_ref,
    offset_ref,
    base_ref,
    charge_ref,
    zh_ref,
    zl_ref,
    zth_ref,
    ztl_ref,
    yh_ref,
    yl_ref,
    yth_ref,
    ytl_ref,
    xh_ref,
    xl_ref,
    xth_ref,
    xtl_ref,
    gain_ref,
    square_ref,
    zfactor_ref,
    send_a,
    recv_a,
    send_b,
    recv_b,
    send_c,
    recv_c,
    send_d,
    recv_d,
    depth_h,
    depth_l,
    atom_h,
    atom_l,
    send_sems,
    recv_sems,
    local_sems,
    ring_sem,
):
    w = lax.axis_index("wide")
    n = lax.axis_index("narrow")
    place = lax.div(w, DOMAINS)
    v = lax.rem(w, DOMAINS)
    core = lax.rem(v, 2)
    y = lax.div(v, 2) * 2 + lax.div(n, 4)
    x = lax.rem(n, 4)
    ys = [lax.rem(y + i, 4) for i in range(4)]
    xs = [lax.rem(x + i, 4) for i in range(4)]
    cores = [core, 1 - core]
    vs = [[lax.div(j, 2) * 2 + c for c in cores] for j in ys]
    ns = [[lax.rem(j, 2) * 4 + i for i in xs] for j in ys]

    def ring_mate(offset):
        other = lax.rem(place + offset, RING)
        return other, (other * DOMAINS + v, n)

    def layer_mate(offset):
        dy, dx, dc = offset
        v_to, n_to = vs[dy][dc], ns[dy][dx]
        return v_to, n_to, (place * DOMAINS + v_to, n_to)

    ring = [o[0] for o in far_first((RING,))]
    layer = far_first((4, 4, 2))

    barrier = pltpu.get_barrier_semaphore()
    inputs = (
        (offset_hbm, offset_ref),
        (base_hbm, base_ref),
        (charge_hbm, charge_ref),
        (zh_hbm, zh_ref),
        (zl_hbm, zl_ref),
        (yth_hbm, yth_ref),
        (ytl_hbm, ytl_ref),
        (zfactor_hbm, zfactor_ref),
        (gain_hbm, gain_ref),
        (square_hbm, square_ref),
        (xh_hbm, xh_ref),
        (xl_hbm, xl_ref),
        (xth_hbm, xth_ref),
        (xtl_hbm, xtl_ref),
        (yh_hbm, yh_ref),
        (yl_hbm, yl_ref),
        (zth_hbm, zth_ref),
        (ztl_hbm, ztl_ref),
    )
    loads = [pltpu.make_async_copy(a, b, local_sems.at[i]) for i, (a, b) in enumerate(inputs)]
    for load in loads[:3]:
        load.start()

    near = [o for o in ring if min(o, RING - o) <= REACH]
    mates = [ring_mate(offset)[1] for offset in near[:2]]
    mates += [layer_mate(offset)[2] for offset in layer]
    mates += [ring_mate(offset)[1] for offset in near[2:]]
    for mate in mates:
        pl.semaphore_signal(barrier, inc=1, device_id=mate, device_id_type=MESH)

    for load in loads[3:]:
        load.start()

    lanes = lax.broadcasted_iota(jnp.int32, (1, 128), 1)
    low_lanes = lanes < HALF
    low_rows = lax.broadcasted_iota(jnp.int32, (1, 8, 1), 1) < CX

    for load in loads[:3]:
        load.wait()
    t = [offset_ref[d, 0] for d in range(3)]
    corner = [base_ref[d, 0] for d in range(3)]
    weights = [spline_weights(u) for u in t]
    slopes = [spline_slopes(u) for u in t]
    occupied = lax.broadcasted_iota(jnp.int32, (1, SLOTS), 1) < count_ref[0, 0]
    charge = jnp.where(occupied, charge_ref[0], 0.0)

    def depth_steps(first):
        cell = lax.broadcasted_iota(jnp.int32, (128, SLOTS), 0) + first
        return (cell - corner[2]) & (NZ - 1)

    for first in range(0, NZ, 128):
        high, low = split(pick(depth_steps(first), weights[2]))
        depth_h[first : first + 128, :SLOTS] = high
        depth_l[first : first + 128, :SLOTS] = low

    row_steps = lax.broadcasted_iota(jnp.int32, (16, SLOTS), 0) - corner[1]
    row_w = pick(row_steps, weights[1])
    row_q = row_w * charge
    plane_w = [pick(p - corner[0], weights[0]) for p in range(PLANES)]
    cross = jnp.concatenate([row_q * plane_w[p] for p in range(PLANES)], axis=0)
    grid = dot3(split(cross), (depth_h[:, :SLOTS], depth_l[:, :SLOTS]), ((1,), (1,)))
    for load in loads[3:5]:
        load.wait()
    spectrum = dot3(split(grid), (zh_ref[...], zl_ref[...]), ((1,), (0,)))
    for m in range(DOMAINS):
        tiles = [spectrum[16 * p : 16 * p + 16, 128 * m : 128 * m + 128] for p in range(PLANES)]
        tiles = exchange_lanes(tiles + [jnp.zeros((16, 128), F32)], lanes)
        for e in range(NARROW):
            send_a[16 * (8 * m + e) : 16 * (8 * m + e) + 16, :] = tiles[e]

    pl.semaphore_wait(barrier, len(near) + len(layer))

    def push(stage, source, target, to):
        pltpu.make_async_remote_copy(
            src_ref=source,
            dst_ref=target,
            send_sem=send_sems.at[stage],
            recv_sem=recv_sems.at[stage],
            device_id=to,
            device_id_type=MESH,
        ).start()

    def drain(stage, block):
        return pltpu.make_async_remote_copy(
            src_ref=block,
            dst_ref=block,
            send_sem=send_sems.at[stage],
            recv_sem=recv_sems.at[stage],
            device_id=(w, n),
            device_id_type=MESH,
        )

    mine = 8 * v + n
    own_a = recv_a.at[pl.ds(ROWS * mine, ROWS)]
    for offset in layer:
        v_to, n_to, to = layer_mate(offset)
        push(0, send_a.at[pl.ds(16 * (8 * v_to + n_to), ROWS)], own_a, to)
    keep_a = pltpu.make_async_copy(send_a.at[pl.ds(16 * mine, ROWS)], own_a, local_sems.at[18])
    keep_a.start()
    for offset in (REACH, RING - REACH):
        pl.semaphore_signal(ring_sem, inc=1, device_id=ring_mate(offset)[1], device_id_type=MESH)

    row_s = pick(row_steps, slopes[1])
    plane_s = [pick(p - corner[0], slopes[0]) for p in range(PLANES)]
    for first in range(0, NZ, 128):
        high, low = split(pick(depth_steps(first), slopes[2]))
        depth_h[first : first + 128, SLOTS:] = high
        depth_l[first : first + 128, SLOTS:] = low
    for load in loads[5:]:
        load.wait()
    coefficient = 128 * v + 8 * place + n
    chosen = lax.broadcasted_iota(jnp.int32, (8, NZ), 1) == coefficient
    zfactor = jnp.sum(jnp.where(chosen, zfactor_ref[...], 0.0), axis=1, keepdims=True)
    squared = square_ref[...] + zfactor[0:1]
    positive = jnp.where(squared > 0.0, squared, 1.0)
    influence = jnp.where(squared > 0.0, gain_ref[...] * zfactor[1:2] / positive, 0.0)

    keep_a.wait()
    drain(0, recv_a.at[pl.ds(0, ROWS * 31)]).wait_recv()
    half = 8 * ROWS * 2
    rows = jnp.concatenate([recv_a[:half], recv_a[half:]], axis=1)
    columns = dot3((yth_ref[...], ytl_ref[...]), split(rows), ((1,), (0,)))
    first = columns[:, :128].T.reshape(RING, 8, 128)
    second = columns[:, 128:].T.reshape(RING, 8, 128)

    def both(value):
        return swap(value.reshape(8 * RING, 128)).reshape(RING, 8, 128)

    def turn(value):
        return pltpu.roll(value, CX, 1)

    first_swapped = both(first)
    second_swapped = both(second)
    low3 = low_lanes.reshape(1, 1, 128)
    upper = first + jnp.where(low3, 0.0, turn(first_swapped))
    lower = turn(second) + jnp.where(low3, first_swapped, second_swapped)
    send_b[:, 0:8, :] = jnp.where(low_rows, upper, lower)
    send_b[:, 8:16, :] = turn(second_swapped)

    pl.semaphore_wait(ring_sem, 2)
    for offset in ring:
        other, to = ring_mate(offset)
        push(1, send_b.at[other, pl.ds(0, 12)], recv_b.at[place, pl.ds(0, 12)], to)
    recv_b[place] = send_b[place]
    for first in range(0, NZ, 128):
        part = slice(first, first + 128)
        z_rows = (zth_ref[part, :], ztl_ref[part, :])
        high, low = split(dot3(z_rows, (depth_h[...], depth_l[...]), ((1,), (0,))))
        atom_h[part, :] = high
        atom_l[part, :] = low
    drain(1, recv_b.at[pl.ds(0, 15), pl.ds(0, 12)]).wait_recv()

    beyond = recv_b[:, 8:16, :]
    beyond = jnp.concatenate([beyond[RING - 1 :], beyond[: RING - 1]], axis=0)
    planes = recv_b[:, 0:8, :] + jnp.where(low_rows & low3, beyond, 0.0)
    planes = planes.reshape(8 * RING, 128)
    turned = swap(planes)
    stacked = jnp.concatenate(
        [jnp.where(low_lanes, planes, turned), jnp.where(low_lanes, turned, planes)], axis=0
    )
    filtered = dot3((xh_ref[...], xl_ref[...]), split(stacked), ((1,), (0,))) * influence
    planes = dot3((xth_ref[...], xtl_ref[...]), split(filtered), ((1,), (0,)))
    planes = jnp.where(low_lanes, planes[:128], planes[128:]).reshape(RING, 8, 128)
    send_c[:, 0:8, :] = planes
    send_c[:, 8:16, :] = jnp.concatenate([planes[1:], planes[:1]], axis=0)

    for offset in ring:
        other, to = ring_mate(offset)
        push(2, send_c.at[other, pl.ds(0, 12)], recv_c.at[place, pl.ds(0, 12)], to)
    recv_c[place] = send_c[place]
    drain(2, recv_c.at[pl.ds(0, 15), pl.ds(0, 12)]).wait_recv()

    own = recv_c[:, 0:8, :]
    own_swapped = both(own)
    beyond = turn(both(recv_c[:, 8:16, :]))
    first = jnp.where(low_rows, own, jnp.where(low3, turn(own_swapped), own_swapped))
    second = jnp.where(low_rows, turn(own), jnp.where(low3, own_swapped, beyond))
    columns = jnp.concatenate([first, second], axis=0).reshape(16 * RING, 128)
    rows = dot3((yh_ref[...], yl_ref[...]), split(columns), ((1,), (1,)))
    send_d[0] = rows[:, :128]
    send_d[1] = rows[:, 128:]

    own_d = recv_d.at[pl.ds(16 * mine, ROWS)]

    def block_d(v_to, n_to):
        return send_d.at[lax.div(v_to, 2), pl.ds(ROWS * (8 * lax.rem(v_to, 2) + n_to), ROWS)]

    for offset in layer:
        v_to, n_to, to = layer_mate(offset)
        push(3, block_d(v_to, n_to), own_d, to)
    keep_d = pltpu.make_async_copy(block_d(v, n), own_d, local_sems.at[19])
    keep_d.start()
    keep_d.wait()
    drain(3, recv_a.at[pl.ds(0, ROWS * 31)]).wait_recv()

    inside = lax.broadcasted_iota(jnp.int32, (16, 128), 0) < ROWS
    parts = []
    for m in range(DOMAINS):
        tiles = [recv_d[16 * (8 * m + e) : 16 * (8 * m + e) + 16, :] for e in range(NARROW)]
        tiles = exchange_lanes([jnp.where(inside, u, 0.0) for u in tiles], lanes)
        parts.append(jnp.concatenate(tiles[:PLANES], axis=0))
    spectrum = jnp.concatenate(parts, axis=1)
    along = dot3(split(spectrum), (atom_h[...], atom_l[...]), ((1,), (0,)))

    total = jnp.zeros((16, SLOTS), F32)
    pull_x, pull_z = total, total
    for p in range(PLANES):
        part = slice(16 * p, 16 * p + 16)
        total = total + along[part, :SLOTS] * plane_w[p]
        pull_x = pull_x + along[part, :SLOTS] * plane_s[p]
        pull_z = pull_z + along[part, SLOTS:] * plane_w[p]

    def over_rows(value):
        return jnp.sum(value, axis=0, keepdims=True)

    factor = factor_ref[0]
    pull_y = over_rows(total * row_s)
    total = over_rows(total * row_w)
    pull_x = over_rows(pull_x * row_w)
    pull_z = over_rows(pull_z * row_w)
    pull = -factor * charge
    raw_ref[0, 0] = pull * pull_x
    raw_ref[1, 0] = pull * pull_y
    raw_ref[2, 0] = pull * pull_z
    raw_ref[3, 0] = jnp.where(occupied, factor * total, 0.0)

    drain(0, recv_a.at[pl.ds(0, ROWS * 31)]).wait_send()
    drain(1, recv_b.at[pl.ds(0, 15), pl.ds(0, 12)]).wait_send()
    drain(2, recv_c.at[pl.ds(0, 15), pl.ds(0, 12)]).wait_send()
    drain(3, recv_a.at[pl.ds(0, ROWS * 31)]).wait_send()


def hand_out(raw_ref, force_ref, grad_ref):
    force_ref[...] = raw_ref[0:3]
    grad_ref[...] = raw_ref[3]


def on_device(offsets, bases, charges, counts, cotangent):
    z_table = real_basis(NZ)[0].T
    y_table = row_matrix()
    x_table = real_basis(NX)[0][:, plane_order()]
    square_x, gain_x = frequency_factors(NX)
    square_y, gain_y = frequency_factors(NY)
    zfactor = np.zeros((8, NZ), np.float32)
    zfactor[0], zfactor[1] = frequency_factors(NZ)
    square = (square_x[:, None] + np.tile(square_y, 2)[None, :]).astype(np.float32)
    gain = (gain_x[:, None] * np.tile(gain_y, 2)[None, :] / math.pi).astype(np.float32)
    arrays = (
        offsets,
        bases,
        charges,
        *halves(z_table),
        *halves(z_table.T),
        *halves(y_table),
        *halves(y_table.T),
        *halves(x_table),
        *halves(x_table.T),
        gain,
        square,
        zfactor,
    )
    smem = pl.BlockSpec(memory_space=pltpu.SMEM)
    hbm = pl.BlockSpec(memory_space=pltpu.HBM)
    vmem = pl.BlockSpec(memory_space=VMEM)
    raw = pl.pallas_call(
        kernel,
        out_shape=jax.ShapeDtypeStruct((4, 1, 1, SLOTS), F32),
        in_specs=[smem] * 2 + [hbm] * len(arrays),
        out_specs=vmem,
        scratch_shapes=[
            *[VMEM(a.shape, a.dtype) for a in arrays],
            VMEM((16 * 32, 128), F32),
            VMEM((ROWS * 32, 128), F32),
            VMEM((RING, 16, 128), F32),
            VMEM((RING, 16, 128), F32),
            VMEM((RING, 16, 128), F32),
            VMEM((RING, 16, 128), F32),
            VMEM((2, ROWS * 16, 128), F32),
            VMEM((16 * 32, 128), F32),
            VMEM((NZ, 2 * SLOTS), BF16),
            VMEM((NZ, 2 * SLOTS), BF16),
            VMEM((NZ, 2 * SLOTS), BF16),
            VMEM((NZ, 2 * SLOTS), BF16),
            pltpu.SemaphoreType.DMA((4,)),
            pltpu.SemaphoreType.DMA((4,)),
            pltpu.SemaphoreType.DMA((len(arrays) + 2,)),
            pltpu.SemaphoreType.REGULAR,
        ],
        compiler_params=pltpu.CompilerParams(
            collective_id=0, has_side_effects=True, vmem_limit_bytes=40 * 1024 * 1024
        ),
        name="ewald",
    )(counts, cotangent, *[pltpu.with_memory_space_constraint(a, pltpu.HBM) for a in arrays])
    return pl.pallas_call(
        hand_out,
        out_shape=(
            jax.ShapeDtypeStruct((3, 1, 1, SLOTS), F32),
            jax.ShapeDtypeStruct((1, 1, SLOTS), F32),
        ),
        in_specs=[vmem],
        out_specs=(vmem, vmem),
        name="hand_out",
    )(pltpu.with_memory_space_constraint(raw, VMEM))


def solution(mesh):
    placed = (
        P(None, "wide", "narrow", None),
        P(None, "wide", "narrow", None),
        P("wide", "narrow", None),
        P("wide", "narrow"),
        P(),
    )
    return jax.shard_map(
        on_device,
        mesh=mesh,
        in_specs=placed,
        out_specs=(P(None, "wide", "narrow", None), P("wide", "narrow", None)),
        check_vma=False,
    )
```

```python
import math

import jax
import jax.numpy as jnp
import ml_dtypes
import numpy as np
from jax import lax
from jax.experimental import pallas as pl
from jax.experimental.pallas import tpu as pltpu
from jax.sharding import PartitionSpec as P

CX = 4
CY = 8
NZ = 512
WIDE = 64
NARROW = 8
NX = CX * WIDE
NY = CY * NARROW
SLOTS = 512
ROWS = CY + 3
RING = 16
DOMAINS = WIDE // RING
PLANES = CX + 3
REACH = RING // 4
HALF = 64
MESH = pl.DeviceIdType.MESH
VMEM = pltpu.VMEM
F32 = jnp.float32
BF16 = jnp.bfloat16


def real_basis(length):
    c = np.arange(length)
    freq = np.where(c <= length // 2, c, length - c)
    phase = (freq[:, None] * c[None, :]) % length * (2.0 * np.pi / length)
    scale = np.where((freq == 0) | (2 * freq == length), 1.0, np.sqrt(2.0)) / np.sqrt(length)
    table = np.where((c <= length // 2)[:, None], np.cos(phase), np.sin(phase)) * scale[:, None]
    return table, freq


def halves(table):
    table = np.asarray(table, np.float32)
    high = table.astype(ml_dtypes.bfloat16)
    low = (table - high.astype(np.float32)).astype(ml_dtypes.bfloat16)
    return high, low


def frequency_factors(length):
    freq = real_basis(length)[1]
    square = (freq / length) ** 2
    spline = 9.0 / (2.0 + np.cos(2.0 * np.pi * freq / length)) ** 2
    return square, np.exp(-(np.pi**2) * square) * spline


def row_matrix():
    basis = real_basis(NY)[0]
    table = np.zeros((2, NARROW, ROWS, 2, NY))
    for half in range(2):
        for n in range(NARROW):
            for r in range(ROWS):
                table[half, n, r, half] = basis[:, (CY * n + r) % NY]
    return table.reshape(2 * NARROW * ROWS, 2 * NY)


def plane_order():
    half, place, other, plane = np.meshgrid(
        np.arange(2), np.arange(RING), np.arange(2), np.arange(CX), indexing="ij"
    )
    return (CX * (DOMAINS * place + 2 * other + half) + plane).reshape(-1)


def split(value):
    high = value.astype(BF16)
    return high, (value - high.astype(F32)).astype(BF16)


def dot3(a, b, contract):
    dims = (contract, ((), ()))
    both = lax.dot_general(
        jnp.concatenate(a, axis=0), b[0], dims, preferred_element_type=F32
    )
    rows = a[0].shape[0]
    return (both[:rows] + both[rows:]) + lax.dot_general(
        a[0], b[1], dims, preferred_element_type=F32
    )


def dot3_wide(a, b):
    columns = b[0].shape[1]
    both = jnp.dot(a[0], jnp.concatenate(b, axis=1), preferred_element_type=F32)
    return (both[:, :columns] + both[:, columns:]) + jnp.dot(
        a[1], b[0], preferred_element_type=F32
    )


def pick(steps, values):
    out = jnp.where(steps == 3, values[3], 0.0)
    for j in (2, 1, 0):
        out = jnp.where(steps == j, values[j], out)
    return out


def spline_weights(t):
    s = 1.0 - t
    square = t * t
    cube = square * t
    return (
        s * s * s / 6.0,
        (3.0 * cube - 6.0 * square + 4.0) / 6.0,
        (-3.0 * cube + 3.0 * square + 3.0 * t + 1.0) / 6.0,
        cube / 6.0,
    )


def spline_slopes(t):
    s = 1.0 - t
    square = t * t
    return (-0.5 * s * s, 1.5 * square - 2.0 * t, -1.5 * square + t + 0.5, 0.5 * square)


def swap(value):
    return pltpu.roll(value, HALF, 1)


def exchange_lanes(blocks, lanes):
    blocks = list(blocks)
    for bit in range(3):
        step = 1 << bit
        clear = (lanes & step) == 0
        for a in range(8):
            if not a & step:
                x, y = blocks[a], blocks[a + step]
                blocks[a] = jnp.where(clear, x, pltpu.roll(y, step, 1))
                blocks[a + step] = jnp.where(clear, pltpu.roll(x, 128 - step, 1), y)
    return blocks


def far_first(sizes):
    offsets = [o for o in np.ndindex(*sizes) if any(o)]

    def hops(offset):
        return sum(min(o, size - o) for o, size in zip(offset, sizes))

    return sorted(offsets, key=lambda o: -hops(o))


def kernel(
    count_ref,
    factor_ref,
    offset_hbm,
    base_hbm,
    charge_hbm,
    zh_hbm,
    zl_hbm,
    zth_hbm,
    ztl_hbm,
    yh_hbm,
    yl_hbm,
    yth_hbm,
    ytl_hbm,
    xh_hbm,
    xl_hbm,
    xth_hbm,
    xtl_hbm,
    gain_hbm,
    square_hbm,
    zfactor_hbm,
    raw_ref,
    offset_ref,
    base_ref,
    charge_ref,
    zh_ref,
    zl_ref,
    zth_ref,
    ztl_ref,
    yh_ref,
    yl_ref,
    yth_ref,
    ytl_ref,
    xh_ref,
    xl_ref,
    xth_ref,
    xtl_ref,
    gain_ref,
    square_ref,
    zfactor_ref,
    send_a,
    recv_a,
    send_b,
    recv_b,
    send_c,
    recv_c,
    send_d,
    recv_d,
    depth_h,
    depth_l,
    atom_h,
    atom_l,
    along_ref,
    send_sems,
    recv_sems,
    local_sems,
    ring_sem,
):
    w = lax.axis_index("wide")
    n = lax.axis_index("narrow")
    place = lax.div(w, DOMAINS)
    v = lax.rem(w, DOMAINS)
    core = lax.rem(v, 2)
    y = lax.div(v, 2) * 2 + lax.div(n, 4)
    x = lax.rem(n, 4)
    ys = [lax.rem(y + i, 4) for i in range(4)]
    xs = [lax.rem(x + i, 4) for i in range(4)]
    cores = [core, 1 - core]
    vs = [[lax.div(j, 2) * 2 + c for c in cores] for j in ys]
    ns = [[lax.rem(j, 2) * 4 + i for i in xs] for j in ys]

    def ring_mate(offset):
        other = lax.rem(place + offset, RING)
        return other, (other * DOMAINS + v, n)

    def layer_mate(offset):
        dy, dx, dc = offset
        v_to, n_to = vs[dy][dc], ns[dy][dx]
        return v_to, n_to, (place * DOMAINS + v_to, n_to)

    ring = [o[0] for o in far_first((RING,))]
    layer = far_first((4, 4, 2))

    barrier = pltpu.get_barrier_semaphore()
    inputs = (
        (offset_hbm, offset_ref),
        (base_hbm, base_ref),
        (charge_hbm, charge_ref),
        (zh_hbm, zh_ref),
        (zl_hbm, zl_ref),
        (yth_hbm, yth_ref),
        (ytl_hbm, ytl_ref),
        (zfactor_hbm, zfactor_ref),
        (gain_hbm, gain_ref),
        (square_hbm, square_ref),
        (xh_hbm, xh_ref),
        (xl_hbm, xl_ref),
        (xth_hbm, xth_ref),
        (xtl_hbm, xtl_ref),
        (yh_hbm, yh_ref),
        (yl_hbm, yl_ref),
        (zth_hbm, zth_ref),
        (ztl_hbm, ztl_ref),
    )
    loads = [pltpu.make_async_copy(a, b, local_sems.at[i]) for i, (a, b) in enumerate(inputs)]
    for load in loads[:3]:
        load.start()

    near = [o for o in ring if min(o, RING - o) <= REACH]
    mates = [ring_mate(offset)[1] for offset in near[:2]]
    mates += [layer_mate(offset)[2] for offset in layer]
    mates += [ring_mate(offset)[1] for offset in near[2:]]
    for mate in mates:
        pl.semaphore_signal(barrier, inc=1, device_id=mate, device_id_type=MESH)

    for load in loads[3:]:
        load.start()

    lanes = lax.broadcasted_iota(jnp.int32, (1, 128), 1)
    low_lanes = lanes < HALF
    low_rows = lax.broadcasted_iota(jnp.int32, (1, 8, 1), 1) < CX

    for load in loads[:3]:
        load.wait()
    t = [offset_ref[d, 0] for d in range(3)]
    corner = [base_ref[d, 0] for d in range(3)]
    weights = [spline_weights(u) for u in t]
    slopes = [spline_slopes(u) for u in t]
    occupied = lax.broadcasted_iota(jnp.int32, (1, SLOTS), 1) < count_ref[0, 0]
    charge = jnp.where(occupied, charge_ref[0], 0.0)

    def depth_steps(first):
        cell = lax.broadcasted_iota(jnp.int32, (128, SLOTS), 0) + first
        return (cell - corner[2]) & (NZ - 1)

    for first in range(0, NZ, 128):
        high, low = split(pick(depth_steps(first), weights[2]))
        depth_h[first : first + 128, :SLOTS] = high
        depth_l[first : first + 128, :SLOTS] = low

    row_steps = lax.broadcasted_iota(jnp.int32, (16, SLOTS), 0) - corner[1]
    row_w = pick(row_steps, weights[1])
    row_q = row_w * charge
    plane_w = [pick(p - corner[0], weights[0]) for p in range(PLANES)]
    cross = jnp.concatenate([row_q * plane_w[p] for p in range(PLANES)], axis=0)
    grid = dot3(split(cross), (depth_h[:, :SLOTS], depth_l[:, :SLOTS]), ((1,), (1,)))
    for load in loads[3:5]:
        load.wait()
    spectrum = dot3(split(grid), (zh_ref[...], zl_ref[...]), ((1,), (0,)))
    for m in range(DOMAINS):
        tiles = [spectrum[16 * p : 16 * p + 16, 128 * m : 128 * m + 128] for p in range(PLANES)]
        tiles = exchange_lanes(tiles + [jnp.zeros((16, 128), F32)], lanes)
        for e in range(NARROW):
            send_a[16 * (8 * m + e) : 16 * (8 * m + e) + 16, :] = tiles[e]

    pl.semaphore_wait(barrier, len(near) + len(layer))

    def push(stage, source, target, to, far=0):
        pltpu.make_async_remote_copy(
            src_ref=source,
            dst_ref=target,
            send_sem=send_sems.at[stage],
            recv_sem=recv_sems.at[stage + far],
            device_id=to,
            device_id_type=MESH,
        ).start()

    def drain(stage, block):
        return pltpu.make_async_remote_copy(
            src_ref=block,
            dst_ref=block,
            send_sem=send_sems.at[stage],
            recv_sem=recv_sems.at[stage],
            device_id=(w, n),
            device_id_type=MESH,
        )

    for offset in (REACH, RING - REACH):
        pl.semaphore_signal(ring_sem, inc=1, device_id=ring_mate(offset)[1], device_id_type=MESH)

    mine = 8 * v + n
    own_a = recv_a.at[pl.ds(ROWS * mine, ROWS)]
    for offset in layer:
        v_to, n_to, to = layer_mate(offset)
        push(0, send_a.at[pl.ds(16 * (8 * v_to + n_to), ROWS)], own_a, to)
    keep_a = pltpu.make_async_copy(send_a.at[pl.ds(16 * mine, ROWS)], own_a, local_sems.at[18])
    keep_a.start()

    row_s = pick(row_steps, slopes[1])
    plane_s = [pick(p - corner[0], slopes[0]) for p in range(PLANES)]
    for first in range(0, NZ, 128):
        high, low = split(pick(depth_steps(first), slopes[2]))
        depth_h[first : first + 128, SLOTS:] = high
        depth_l[first : first + 128, SLOTS:] = low
    for load in loads[5:]:
        load.wait()
    coefficient = 128 * v + 8 * place + n
    chosen = lax.broadcasted_iota(jnp.int32, (8, NZ), 1) == coefficient
    zfactor = jnp.sum(jnp.where(chosen, zfactor_ref[...], 0.0), axis=1, keepdims=True)
    squared = square_ref[...] + zfactor[0:1]
    positive = jnp.where(squared > 0.0, squared, 1.0)
    influence = jnp.where(squared > 0.0, gain_ref[...] * zfactor[1:2] / positive, 0.0)

    keep_a.wait()
    drain(0, recv_a.at[pl.ds(0, ROWS * 31)]).wait_recv()
    half = 8 * ROWS * 2
    rows = jnp.concatenate([recv_a[:half], recv_a[half:]], axis=1)
    columns = dot3((yth_ref[...], ytl_ref[...]), split(rows), ((1,), (0,)))
    first = columns[:, :128].T.reshape(RING, 8, 128)
    second = columns[:, 128:].T.reshape(RING, 8, 128)

    def both(value):
        return swap(value.reshape(8 * RING, 128)).reshape(RING, 8, 128)

    def turn(value):
        return pltpu.roll(value, CX, 1)

    first_swapped = both(first)
    second_swapped = both(second)
    low3 = low_lanes.reshape(1, 1, 128)
    upper = first + jnp.where(low3, 0.0, turn(first_swapped))
    lower = turn(second) + jnp.where(low3, first_swapped, second_swapped)
    send_b[:, 0:8, :] = jnp.where(low_rows, upper, lower)
    send_b[:, 8:16, :] = turn(second_swapped)

    pl.semaphore_wait(ring_sem, 2)
    for offset in ring:
        other, to = ring_mate(offset)
        push(1, send_b.at[other, pl.ds(0, 12)], recv_b.at[place, pl.ds(0, 12)], to)
    recv_b[place] = send_b[place]
    for first in range(0, NZ, 128):
        part = slice(first, first + 128)
        z_rows = (zth_ref[part, :], ztl_ref[part, :])
        high, low = split(dot3(z_rows, (depth_h[...], depth_l[...]), ((1,), (0,))))
        atom_h[part, :] = high
        atom_l[part, :] = low
    drain(1, recv_b.at[pl.ds(0, 15), pl.ds(0, 12)]).wait_recv()

    beyond = recv_b[:, 8:16, :]
    beyond = jnp.concatenate([beyond[RING - 1 :], beyond[: RING - 1]], axis=0)
    planes = recv_b[:, 0:8, :] + jnp.where(low_rows & low3, beyond, 0.0)
    planes = planes.reshape(8 * RING, 128)
    turned = swap(planes)
    stacked = jnp.concatenate(
        [jnp.where(low_lanes, planes, turned), jnp.where(low_lanes, turned, planes)], axis=0
    )
    filtered = dot3_wide((xh_ref[...], xl_ref[...]), split(stacked)) * influence
    planes = dot3_wide((xth_ref[...], xtl_ref[...]), split(filtered))
    planes = jnp.where(low_lanes, planes[:128], planes[128:]).reshape(RING, 8, 128)
    send_c[:, 0:8, :] = planes
    send_c[:, 8:16, :] = jnp.concatenate([planes[1:], planes[:1]], axis=0)

    for offset in ring:
        other, to = ring_mate(offset)
        push(2, send_c.at[other, pl.ds(0, 12)], recv_c.at[place, pl.ds(0, 12)], to)
    recv_c[place] = send_c[place]
    drain(2, recv_c.at[pl.ds(0, 15), pl.ds(0, 12)]).wait_recv()

    own = recv_c[:, 0:8, :]
    own_swapped = both(own)
    beyond = turn(both(recv_c[:, 8:16, :]))
    first = jnp.where(low_rows, own, jnp.where(low3, turn(own_swapped), own_swapped))
    second = jnp.where(low_rows, turn(own), jnp.where(low3, own_swapped, beyond))
    columns = jnp.concatenate([first, second], axis=0).reshape(16 * RING, 128)
    rows = dot3((yh_ref[...], yl_ref[...]), split(columns), ((1,), (1,)))
    send_d[0] = rows[:, :128]
    send_d[1] = rows[:, 128:]

    own_d = recv_d.at[pl.ds(16 * mine, ROWS)]

    def block_d(v_to, n_to):
        return send_d.at[lax.div(v_to, 2), pl.ds(ROWS * (8 * lax.rem(v_to, 2) + n_to), ROWS)]

    for offset in layer:
        v_to, n_to, to = layer_mate(offset)
        far = lax.rem(lax.div(v_to, 2) + lax.div(v, 2), 2)
        push(3, block_d(v_to, n_to), own_d, to, far)
    keep_d = pltpu.make_async_copy(block_d(v, n), own_d, local_sems.at[19])
    keep_d.start()

    inside = lax.broadcasted_iota(jnp.int32, (16, 128), 0) < ROWS

    def along_half(which):
        parts = []
        for m in range(2):
            start = 256 * which + 128 * m
            tiles = [recv_d[pl.ds(start + 16 * e, 16), :] for e in range(NARROW)]
            tiles = exchange_lanes([jnp.where(inside, u, 0.0) for u in tiles], lanes)
            parts.append(jnp.concatenate(tiles[:PLANES], axis=0))
        spectrum = split(jnp.concatenate(parts, axis=1))
        start = pl.multiple_of(256 * which, 256)
        atoms = (atom_h[pl.ds(start, 256), :], atom_l[pl.ds(start, 256), :])
        return dot3(spectrum, atoms, ((1,), (0,)))

    keep_d.wait()
    drain(3, recv_a.at[pl.ds(0, ROWS * 15)]).wait_recv()
    along_ref[...] = along_half(lax.div(v, 2))
    drain(4, recv_a.at[pl.ds(0, ROWS * 16)]).wait_recv()
    along = along_ref[...] + along_half(1 - lax.div(v, 2))

    total = jnp.zeros((16, SLOTS), F32)
    pull_x, pull_z = total, total
    for p in range(PLANES):
        part = slice(16 * p, 16 * p + 16)
        total = total + along[part, :SLOTS] * plane_w[p]
        pull_x = pull_x + along[part, :SLOTS] * plane_s[p]
        pull_z = pull_z + along[part, SLOTS:] * plane_w[p]

    def over_rows(value):
        return jnp.sum(value, axis=0, keepdims=True)

    factor = factor_ref[0]
    pull_y = over_rows(total * row_s)
    total = over_rows(total * row_w)
    pull_x = over_rows(pull_x * row_w)
    pull_z = over_rows(pull_z * row_w)
    pull = -factor * charge
    raw_ref[0, 0] = pull * pull_x
    raw_ref[1, 0] = pull * pull_y
    raw_ref[2, 0] = pull * pull_z
    raw_ref[3, 0] = jnp.where(occupied, factor * total, 0.0)

    drain(0, recv_a.at[pl.ds(0, ROWS * 31)]).wait_send()
    drain(1, recv_b.at[pl.ds(0, 15), pl.ds(0, 12)]).wait_send()
    drain(2, recv_c.at[pl.ds(0, 15), pl.ds(0, 12)]).wait_send()
    drain(3, recv_a.at[pl.ds(0, ROWS * 31)]).wait_send()


def hand_out(raw_ref, force_ref, grad_ref):
    force_ref[...] = raw_ref[0:3]
    grad_ref[...] = raw_ref[3]


def on_device(offsets, bases, charges, counts, cotangent):
    z_table = real_basis(NZ)[0].T
    y_table = row_matrix()
    x_table = real_basis(NX)[0][:, plane_order()]
    square_x, gain_x = frequency_factors(NX)
    square_y, gain_y = frequency_factors(NY)
    zfactor = np.zeros((8, NZ), np.float32)
    zfactor[0], zfactor[1] = frequency_factors(NZ)
    square = (square_x[:, None] + np.tile(square_y, 2)[None, :]).astype(np.float32)
    gain = (gain_x[:, None] * np.tile(gain_y, 2)[None, :] / math.pi).astype(np.float32)
    arrays = (
        offsets,
        bases,
        charges,
        *halves(z_table),
        *halves(z_table.T),
        *halves(y_table),
        *halves(y_table.T),
        *halves(x_table),
        *halves(x_table.T),
        gain,
        square,
        zfactor,
    )
    smem = pl.BlockSpec(memory_space=pltpu.SMEM)
    hbm = pl.BlockSpec(memory_space=pltpu.HBM)
    vmem = pl.BlockSpec(memory_space=VMEM)
    raw = pl.pallas_call(
        kernel,
        out_shape=jax.ShapeDtypeStruct((4, 1, 1, SLOTS), F32),
        in_specs=[smem] * 2 + [hbm] * len(arrays),
        out_specs=vmem,
        scratch_shapes=[
            *[VMEM(a.shape, a.dtype) for a in arrays],
            VMEM((16 * 32, 128), F32),
            VMEM((ROWS * 32, 128), F32),
            VMEM((RING, 16, 128), F32),
            VMEM((RING, 16, 128), F32),
            VMEM((RING, 16, 128), F32),
            VMEM((RING, 16, 128), F32),
            VMEM((2, ROWS * 16, 128), F32),
            VMEM((16 * 32, 128), F32),
            VMEM((NZ, 2 * SLOTS), BF16),
            VMEM((NZ, 2 * SLOTS), BF16),
            VMEM((NZ, 2 * SLOTS), BF16),
            VMEM((NZ, 2 * SLOTS), BF16),
            VMEM((16 * PLANES, 2 * SLOTS), F32),
            pltpu.SemaphoreType.DMA((4,)),
            pltpu.SemaphoreType.DMA((5,)),
            pltpu.SemaphoreType.DMA((len(arrays) + 2,)),
            pltpu.SemaphoreType.REGULAR,
        ],
        compiler_params=pltpu.CompilerParams(
            collective_id=0, has_side_effects=True, vmem_limit_bytes=40 * 1024 * 1024
        ),
        name="ewald",
    )(counts, cotangent, *[pltpu.with_memory_space_constraint(a, pltpu.HBM) for a in arrays])
    return pl.pallas_call(
        hand_out,
        out_shape=(
            jax.ShapeDtypeStruct((3, 1, 1, SLOTS), F32),
            jax.ShapeDtypeStruct((1, 1, SLOTS), F32),
        ),
        in_specs=[vmem],
        out_specs=(vmem, vmem),
        name="hand_out",
    )(pltpu.with_memory_space_constraint(raw, VMEM))


def solution(mesh):
    placed = (
        P(None, "wide", "narrow", None),
        P(None, "wide", "narrow", None),
        P("wide", "narrow", None),
        P("wide", "narrow"),
        P(),
    )
    return jax.shard_map(
        on_device,
        mesh=mesh,
        in_specs=placed,
        out_specs=(P(None, "wide", "narrow", None), P("wide", "narrow", None)),
        check_vma=False,
    )
```

```python
import math

import jax
import jax.numpy as jnp
import ml_dtypes
import numpy as np
from jax import lax
from jax.experimental import pallas as pl
from jax.experimental.pallas import tpu as pltpu
from jax.sharding import PartitionSpec as P

CX = 4
CY = 8
NZ = 512
WIDE = 64
NARROW = 8
NX = CX * WIDE
NY = CY * NARROW
SLOTS = 512
ROWS = CY + 3
RING = 16
DOMAINS = WIDE // RING
PLANES = CX + 3
REACH = RING // 4
HALF = 64
MESH = pl.DeviceIdType.MESH
VMEM = pltpu.VMEM
F32 = jnp.float32
BF16 = jnp.bfloat16


def real_basis(length):
    c = np.arange(length)
    freq = np.where(c <= length // 2, c, length - c)
    phase = (freq[:, None] * c[None, :]) % length * (2.0 * np.pi / length)
    scale = np.where((freq == 0) | (2 * freq == length), 1.0, np.sqrt(2.0)) / np.sqrt(length)
    table = np.where((c <= length // 2)[:, None], np.cos(phase), np.sin(phase)) * scale[:, None]
    return table, freq


def halves(table):
    table = np.asarray(table, np.float32)
    high = table.astype(ml_dtypes.bfloat16)
    low = (table - high.astype(np.float32)).astype(ml_dtypes.bfloat16)
    return high, low


def frequency_factors(length):
    freq = real_basis(length)[1]
    square = (freq / length) ** 2
    spline = 9.0 / (2.0 + np.cos(2.0 * np.pi * freq / length)) ** 2
    return square, np.exp(-(np.pi**2) * square) * spline


def row_matrix():
    basis = real_basis(NY)[0]
    table = np.zeros((2, NARROW, ROWS, 2, NY))
    for half in range(2):
        for n in range(NARROW):
            for r in range(ROWS):
                table[half, n, r, half] = basis[:, (CY * n + r) % NY]
    return table.reshape(2 * NARROW * ROWS, 2 * NY)


def plane_order():
    half, place, other, plane = np.meshgrid(
        np.arange(2), np.arange(RING), np.arange(2), np.arange(CX), indexing="ij"
    )
    return (CX * (DOMAINS * place + 2 * other + half) + plane).reshape(-1)


def split(value):
    high = value.astype(BF16)
    return high, (value - high.astype(F32)).astype(BF16)


def dot3(a, b, contract):
    dims = (contract, ((), ()))
    both = lax.dot_general(
        jnp.concatenate(a, axis=0), b[0], dims, preferred_element_type=F32
    )
    rows = a[0].shape[0]
    return (both[:rows] + both[rows:]) + lax.dot_general(
        a[0], b[1], dims, preferred_element_type=F32
    )


def dot3_wide(a, b):
    columns = b[0].shape[1]
    both = jnp.dot(a[0], jnp.concatenate(b, axis=1), preferred_element_type=F32)
    return (both[:, :columns] + both[:, columns:]) + jnp.dot(
        a[1], b[0], preferred_element_type=F32
    )


def pick(steps, values):
    out = jnp.where(steps == 3, values[3], 0.0)
    for j in (2, 1, 0):
        out = jnp.where(steps == j, values[j], out)
    return out


def spline_weights(t):
    s = 1.0 - t
    square = t * t
    cube = square * t
    return (
        s * s * s / 6.0,
        (3.0 * cube - 6.0 * square + 4.0) / 6.0,
        (-3.0 * cube + 3.0 * square + 3.0 * t + 1.0) / 6.0,
        cube / 6.0,
    )


def spline_slopes(t):
    s = 1.0 - t
    square = t * t
    return (-0.5 * s * s, 1.5 * square - 2.0 * t, -1.5 * square + t + 0.5, 0.5 * square)


def swap(value):
    return pltpu.roll(value, HALF, 1)


def exchange_lanes(blocks, lanes):
    blocks = list(blocks)
    for bit in range(3):
        step = 1 << bit
        clear = (lanes & step) == 0
        for a in range(8):
            if not a & step:
                x, y = blocks[a], blocks[a + step]
                blocks[a] = jnp.where(clear, x, pltpu.roll(y, step, 1))
                blocks[a + step] = jnp.where(clear, pltpu.roll(x, 128 - step, 1), y)
    return blocks


def far_first(sizes):
    offsets = [o for o in np.ndindex(*sizes) if any(o)]

    def hops(offset):
        return sum(min(o, size - o) for o, size in zip(offset, sizes))

    return sorted(offsets, key=lambda o: (-hops(o), o[-1], o[0] % 2))


def kernel(
    count_ref,
    factor_ref,
    offset_hbm,
    base_hbm,
    charge_hbm,
    zh_hbm,
    zl_hbm,
    zth_hbm,
    ztl_hbm,
    yh_hbm,
    yl_hbm,
    yth_hbm,
    ytl_hbm,
    xh_hbm,
    xl_hbm,
    xth_hbm,
    xtl_hbm,
    gain_hbm,
    square_hbm,
    zfactor_hbm,
    raw_ref,
    offset_ref,
    base_ref,
    charge_ref,
    zh_ref,
    zl_ref,
    zth_ref,
    ztl_ref,
    yh_ref,
    yl_ref,
    yth_ref,
    ytl_ref,
    xh_ref,
    xl_ref,
    xth_ref,
    xtl_ref,
    gain_ref,
    square_ref,
    zfactor_ref,
    send_a,
    recv_a,
    send_b,
    recv_b,
    send_c,
    recv_c,
    send_d,
    recv_d,
    depth_h,
    depth_l,
    atom_h,
    atom_l,
    along_ref,
    send_sems,
    recv_sems,
    local_sems,
    ring_sem,
):
    w = lax.axis_index("wide")
    n = lax.axis_index("narrow")
    place = lax.div(w, DOMAINS)
    v = lax.rem(w, DOMAINS)
    core = lax.rem(v, 2)
    y = lax.div(v, 2) * 2 + lax.div(n, 4)
    x = lax.rem(n, 4)
    ys = [lax.rem(y + i, 4) for i in range(4)]
    xs = [lax.rem(x + i, 4) for i in range(4)]
    cores = [core, 1 - core]
    vs = [[lax.div(j, 2) * 2 + c for c in cores] for j in ys]
    ns = [[lax.rem(j, 2) * 4 + i for i in xs] for j in ys]

    def ring_mate(offset):
        other = lax.rem(place + offset, RING)
        return other, (other * DOMAINS + v, n)

    def layer_mate(offset):
        dy, dx, dc = offset
        v_to, n_to = vs[dy][dc], ns[dy][dx]
        return v_to, n_to, (place * DOMAINS + v_to, n_to)

    ring = [o[0] for o in far_first((RING,))]
    layer = far_first((4, 4, 2))

    barrier = pltpu.get_barrier_semaphore()
    inputs = (
        (offset_hbm, offset_ref),
        (base_hbm, base_ref),
        (charge_hbm, charge_ref),
        (zh_hbm, zh_ref),
        (zl_hbm, zl_ref),
        (yth_hbm, yth_ref),
        (ytl_hbm, ytl_ref),
        (zfactor_hbm, zfactor_ref),
        (gain_hbm, gain_ref),
        (square_hbm, square_ref),
        (xh_hbm, xh_ref),
        (xl_hbm, xl_ref),
        (xth_hbm, xth_ref),
        (xtl_hbm, xtl_ref),
        (yh_hbm, yh_ref),
        (yl_hbm, yl_ref),
        (zth_hbm, zth_ref),
        (ztl_hbm, ztl_ref),
    )
    loads = [pltpu.make_async_copy(a, b, local_sems.at[i]) for i, (a, b) in enumerate(inputs)]
    for load in loads[:3]:
        load.start()

    near = [o for o in ring if min(o, RING - o) <= REACH]
    mates = [ring_mate(offset)[1] for offset in near[:2]]
    mates += [layer_mate(offset)[2] for offset in layer]
    mates += [ring_mate(offset)[1] for offset in near[2:]]
    for mate in mates:
        pl.semaphore_signal(barrier, inc=1, device_id=mate, device_id_type=MESH)

    for load in loads[3:]:
        load.start()

    lanes = lax.broadcasted_iota(jnp.int32, (1, 128), 1)
    low_lanes = lanes < HALF
    low_rows = lax.broadcasted_iota(jnp.int32, (1, 8, 1), 1) < CX

    for load in loads[:3]:
        load.wait()
    t = [offset_ref[d, 0] for d in range(3)]
    corner = [base_ref[d, 0] for d in range(3)]
    weights = [spline_weights(u) for u in t]
    slopes = [spline_slopes(u) for u in t]
    occupied = lax.broadcasted_iota(jnp.int32, (1, SLOTS), 1) < count_ref[0, 0]
    charge = jnp.where(occupied, charge_ref[0], 0.0)

    def depth_steps(first):
        cell = lax.broadcasted_iota(jnp.int32, (128, SLOTS), 0) + first
        return (cell - corner[2]) & (NZ - 1)

    for first in range(0, NZ, 128):
        high, low = split(pick(depth_steps(first), weights[2]))
        depth_h[first : first + 128, :SLOTS] = high
        depth_l[first : first + 128, :SLOTS] = low

    row_steps = lax.broadcasted_iota(jnp.int32, (16, SLOTS), 0) - corner[1]
    row_w = pick(row_steps, weights[1])
    row_q = row_w * charge
    plane_w = [pick(p - corner[0], weights[0]) for p in range(PLANES)]
    cross = jnp.concatenate([row_q * plane_w[p] for p in range(PLANES)], axis=0)
    grid = dot3(split(cross), (depth_h[:, :SLOTS], depth_l[:, :SLOTS]), ((1,), (1,)))
    for load in loads[3:5]:
        load.wait()
    spectrum = dot3(split(grid), (zh_ref[...], zl_ref[...]), ((1,), (0,)))
    for m in range(DOMAINS):
        tiles = [spectrum[16 * p : 16 * p + 16, 128 * m : 128 * m + 128] for p in range(PLANES)]
        tiles = exchange_lanes(tiles + [jnp.zeros((16, 128), F32)], lanes)
        for e in range(NARROW):
            send_a[16 * (8 * m + e) : 16 * (8 * m + e) + 16, :] = tiles[e]

    pl.semaphore_wait(barrier, len(near) + len(layer))

    def push(stage, source, target, to, far=0):
        pltpu.make_async_remote_copy(
            src_ref=source,
            dst_ref=target,
            send_sem=send_sems.at[stage],
            recv_sem=recv_sems.at[stage + far],
            device_id=to,
            device_id_type=MESH,
        ).start()

    def drain(stage, block):
        return pltpu.make_async_remote_copy(
            src_ref=block,
            dst_ref=block,
            send_sem=send_sems.at[stage],
            recv_sem=recv_sems.at[stage],
            device_id=(w, n),
            device_id_type=MESH,
        )

    for offset in (REACH, RING - REACH):
        pl.semaphore_signal(ring_sem, inc=1, device_id=ring_mate(offset)[1], device_id_type=MESH)

    mine = 8 * v + n
    own_a = recv_a.at[pl.ds(ROWS * mine, ROWS)]
    for offset in layer:
        v_to, n_to, to = layer_mate(offset)
        push(0, send_a.at[pl.ds(16 * (8 * v_to + n_to), ROWS)], own_a, to)
    keep_a = pltpu.make_async_copy(send_a.at[pl.ds(16 * mine, ROWS)], own_a, local_sems.at[18])
    keep_a.start()

    row_s = pick(row_steps, slopes[1])
    plane_s = [pick(p - corner[0], slopes[0]) for p in range(PLANES)]
    for first in range(0, NZ, 128):
        high, low = split(pick(depth_steps(first), slopes[2]))
        depth_h[first : first + 128, SLOTS:] = high
        depth_l[first : first + 128, SLOTS:] = low
    for load in loads[5:]:
        load.wait()
    coefficient = 128 * v + 8 * place + n
    chosen = lax.broadcasted_iota(jnp.int32, (8, NZ), 1) == coefficient
    zfactor = jnp.sum(jnp.where(chosen, zfactor_ref[...], 0.0), axis=1, keepdims=True)
    squared = square_ref[...] + zfactor[0:1]
    positive = jnp.where(squared > 0.0, squared, 1.0)
    influence = jnp.where(squared > 0.0, gain_ref[...] * zfactor[1:2] / positive, 0.0)

    keep_a.wait()
    drain(0, recv_a.at[pl.ds(0, ROWS * 31)]).wait_recv()
    half = 8 * ROWS * 2
    rows = jnp.concatenate([recv_a[:half], recv_a[half:]], axis=1)
    columns = dot3((yth_ref[...], ytl_ref[...]), split(rows), ((1,), (0,)))
    first = columns[:, :128].T.reshape(RING, 8, 128)
    second = columns[:, 128:].T.reshape(RING, 8, 128)

    def both(value):
        return swap(value.reshape(8 * RING, 128)).reshape(RING, 8, 128)

    def turn(value):
        return pltpu.roll(value, CX, 1)

    first_swapped = both(first)
    second_swapped = both(second)
    low3 = low_lanes.reshape(1, 1, 128)
    upper = first + jnp.where(low3, 0.0, turn(first_swapped))
    lower = turn(second) + jnp.where(low3, first_swapped, second_swapped)
    send_b[:, 0:8, :] = jnp.where(low_rows, upper, lower)
    send_b[:, 8:16, :] = turn(second_swapped)

    pl.semaphore_wait(ring_sem, 2)
    for offset in ring:
        other, to = ring_mate(offset)
        push(1, send_b.at[other, pl.ds(0, 12)], recv_b.at[place, pl.ds(0, 12)], to)
    recv_b[place] = send_b[place]
    for first in range(0, NZ, 128):
        part = slice(first, first + 128)
        z_rows = (zth_ref[part, :], ztl_ref[part, :])
        high, low = split(dot3(z_rows, (depth_h[...], depth_l[...]), ((1,), (0,))))
        atom_h[part, :] = high
        atom_l[part, :] = low
    drain(1, recv_b.at[pl.ds(0, 15), pl.ds(0, 12)]).wait_recv()

    beyond = recv_b[:, 8:16, :]
    beyond = jnp.concatenate([beyond[RING - 1 :], beyond[: RING - 1]], axis=0)
    planes = recv_b[:, 0:8, :] + jnp.where(low_rows & low3, beyond, 0.0)
    planes = planes.reshape(8 * RING, 128)
    turned = swap(planes)
    stacked = jnp.concatenate(
        [jnp.where(low_lanes, planes, turned), jnp.where(low_lanes, turned, planes)], axis=0
    )
    filtered = dot3_wide((xh_ref[...], xl_ref[...]), split(stacked)) * influence
    planes = dot3_wide((xth_ref[...], xtl_ref[...]), split(filtered))
    planes = jnp.where(low_lanes, planes[:128], planes[128:]).reshape(RING, 8, 128)
    send_c[:, 0:8, :] = planes
    send_c[:, 8:16, :] = jnp.concatenate([planes[1:], planes[:1]], axis=0)

    for offset in ring:
        other, to = ring_mate(offset)
        push(2, send_c.at[other, pl.ds(0, 12)], recv_c.at[place, pl.ds(0, 12)], to)
    recv_c[place] = send_c[place]
    drain(2, recv_c.at[pl.ds(0, 15), pl.ds(0, 12)]).wait_recv()

    own = recv_c[:, 0:8, :]
    own_swapped = both(own)
    beyond = turn(both(recv_c[:, 8:16, :]))
    first = jnp.where(low_rows, own, jnp.where(low3, turn(own_swapped), own_swapped))
    second = jnp.where(low_rows, turn(own), jnp.where(low3, own_swapped, beyond))
    columns = jnp.concatenate([first, second], axis=0).reshape(16 * RING, 128)
    rows = dot3((yh_ref[...], yl_ref[...]), split(columns), ((1,), (1,)))
    send_d[0] = rows[:, :128]
    send_d[1] = rows[:, 128:]

    own_d = recv_d.at[pl.ds(16 * mine, ROWS)]

    def block_d(v_to, n_to):
        return send_d.at[lax.div(v_to, 2), pl.ds(ROWS * (8 * lax.rem(v_to, 2) + n_to), ROWS)]

    for offset in layer:
        v_to, n_to, to = layer_mate(offset)
        far = lax.rem(lax.div(v_to, 2) + lax.div(v, 2), 2)
        push(3, block_d(v_to, n_to), own_d, to, far)
    keep_d = pltpu.make_async_copy(block_d(v, n), own_d, local_sems.at[19])
    keep_d.start()

    inside = lax.broadcasted_iota(jnp.int32, (16, 128), 0) < ROWS

    def along_half(which):
        parts = []
        for m in range(2):
            start = 256 * which + 128 * m
            tiles = [recv_d[pl.ds(start + 16 * e, 16), :] for e in range(NARROW)]
            tiles = exchange_lanes([jnp.where(inside, u, 0.0) for u in tiles], lanes)
            parts.append(jnp.concatenate(tiles[:PLANES], axis=0))
        spectrum = split(jnp.concatenate(parts, axis=1))
        start = pl.multiple_of(256 * which, 256)
        atoms = (atom_h[pl.ds(start, 256), :], atom_l[pl.ds(start, 256), :])
        return dot3(spectrum, atoms, ((1,), (0,)))

    keep_d.wait()
    drain(3, recv_a.at[pl.ds(0, ROWS * 15)]).wait_recv()
    along_ref[...] = along_half(lax.div(v, 2))
    drain(4, recv_a.at[pl.ds(0, ROWS * 16)]).wait_recv()
    along = along_ref[...] + along_half(1 - lax.div(v, 2))

    total = jnp.zeros((16, SLOTS), F32)
    pull_x, pull_z = total, total
    for p in range(PLANES):
        part = slice(16 * p, 16 * p + 16)
        total = total + along[part, :SLOTS] * plane_w[p]
        pull_x = pull_x + along[part, :SLOTS] * plane_s[p]
        pull_z = pull_z + along[part, SLOTS:] * plane_w[p]

    def over_rows(value):
        return jnp.sum(value, axis=0, keepdims=True)

    factor = factor_ref[0]
    pull_y = over_rows(total * row_s)
    total = over_rows(total * row_w)
    pull_x = over_rows(pull_x * row_w)
    pull_z = over_rows(pull_z * row_w)
    pull = -factor * charge
    raw_ref[0, 0] = pull * pull_x
    raw_ref[1, 0] = pull * pull_y
    raw_ref[2, 0] = pull * pull_z
    raw_ref[3, 0] = jnp.where(occupied, factor * total, 0.0)

    drain(0, recv_a.at[pl.ds(0, ROWS * 31)]).wait_send()
    drain(1, recv_b.at[pl.ds(0, 15), pl.ds(0, 12)]).wait_send()
    drain(2, recv_c.at[pl.ds(0, 15), pl.ds(0, 12)]).wait_send()
    drain(3, recv_a.at[pl.ds(0, ROWS * 31)]).wait_send()


def hand_out(raw_ref, force_hbm, grad_hbm, sems):
    forces = pltpu.make_async_copy(raw_ref.at[pl.ds(0, 3)], force_hbm, sems.at[0])
    grads = pltpu.make_async_copy(raw_ref.at[3], grad_hbm, sems.at[1])
    forces.start()
    grads.start()
    forces.wait()
    grads.wait()


def on_device(offsets, bases, charges, counts, cotangent):
    z_table = real_basis(NZ)[0].T
    y_table = row_matrix()
    x_table = real_basis(NX)[0][:, plane_order()]
    square_x, gain_x = frequency_factors(NX)
    square_y, gain_y = frequency_factors(NY)
    zfactor = np.zeros((8, NZ), np.float32)
    zfactor[0], zfactor[1] = frequency_factors(NZ)
    square = (square_x[:, None] + np.tile(square_y, 2)[None, :]).astype(np.float32)
    gain = (gain_x[:, None] * np.tile(gain_y, 2)[None, :] / math.pi).astype(np.float32)
    arrays = (
        offsets,
        bases,
        charges,
        *halves(z_table),
        *halves(z_table.T),
        *halves(y_table),
        *halves(y_table.T),
        *halves(x_table),
        *halves(x_table.T),
        gain,
        square,
        zfactor,
    )
    smem = pl.BlockSpec(memory_space=pltpu.SMEM)
    hbm = pl.BlockSpec(memory_space=pltpu.HBM)
    vmem = pl.BlockSpec(memory_space=VMEM)
    raw = pl.pallas_call(
        kernel,
        out_shape=jax.ShapeDtypeStruct((4, 1, 1, SLOTS), F32),
        in_specs=[smem] * 2 + [hbm] * len(arrays),
        out_specs=vmem,
        scratch_shapes=[
            *[VMEM(a.shape, a.dtype) for a in arrays],
            VMEM((16 * 32, 128), F32),
            VMEM((ROWS * 32, 128), F32),
            VMEM((RING, 16, 128), F32),
            VMEM((RING, 16, 128), F32),
            VMEM((RING, 16, 128), F32),
            VMEM((RING, 16, 128), F32),
            VMEM((2, ROWS * 16, 128), F32),
            VMEM((16 * 32, 128), F32),
            VMEM((NZ, 2 * SLOTS), BF16),
            VMEM((NZ, 2 * SLOTS), BF16),
            VMEM((NZ, 2 * SLOTS), BF16),
            VMEM((NZ, 2 * SLOTS), BF16),
            VMEM((16 * PLANES, 2 * SLOTS), F32),
            pltpu.SemaphoreType.DMA((4,)),
            pltpu.SemaphoreType.DMA((5,)),
            pltpu.SemaphoreType.DMA((len(arrays) + 2,)),
            pltpu.SemaphoreType.REGULAR,
        ],
        compiler_params=pltpu.CompilerParams(
            collective_id=0, has_side_effects=True, vmem_limit_bytes=40 * 1024 * 1024
        ),
        name="ewald",
    )(counts, cotangent, *[pltpu.with_memory_space_constraint(a, pltpu.HBM) for a in arrays])
    return pl.pallas_call(
        hand_out,
        out_shape=(
            jax.ShapeDtypeStruct((3, 1, 1, SLOTS), F32),
            jax.ShapeDtypeStruct((1, 1, SLOTS), F32),
        ),
        in_specs=[vmem],
        out_specs=(hbm, hbm),
        scratch_shapes=[pltpu.SemaphoreType.DMA((2,))],
        name="hand_out",
    )(pltpu.with_memory_space_constraint(raw, VMEM))


def solution(mesh):
    placed = (
        P(None, "wide", "narrow", None),
        P(None, "wide", "narrow", None),
        P("wide", "narrow", None),
        P("wide", "narrow"),
        P(),
    )
    return jax.shard_map(
        on_device,
        mesh=mesh,
        in_specs=placed,
        out_specs=(P(None, "wide", "narrow", None), P("wide", "narrow", None)),
        check_vma=False,
    )
```

```python
import math

import jax
import jax.numpy as jnp
import ml_dtypes
import numpy as np
from jax import lax
from jax.experimental import pallas as pl
from jax.experimental.pallas import tpu as pltpu
from jax.sharding import PartitionSpec as P

CX = 4
CY = 8
NZ = 512
WIDE = 64
NARROW = 8
NX = CX * WIDE
NY = CY * NARROW
SLOTS = 512
ROWS = CY + 3
RING = 16
DOMAINS = WIDE // RING
PLANES = CX + 3
REACH = RING // 4
HALF = 64
MESH = pl.DeviceIdType.MESH
VMEM = pltpu.VMEM
F32 = jnp.float32
BF16 = jnp.bfloat16


def real_basis(length):
    c = np.arange(length)
    freq = np.where(c <= length // 2, c, length - c)
    phase = (freq[:, None] * c[None, :]) % length * (2.0 * np.pi / length)
    scale = np.where((freq == 0) | (2 * freq == length), 1.0, np.sqrt(2.0)) / np.sqrt(length)
    table = np.where((c <= length // 2)[:, None], np.cos(phase), np.sin(phase)) * scale[:, None]
    return table, freq


def halves(table):
    table = np.asarray(table, np.float32)
    high = table.astype(ml_dtypes.bfloat16)
    low = (table - high.astype(np.float32)).astype(ml_dtypes.bfloat16)
    return high, low


def frequency_factors(length):
    freq = real_basis(length)[1]
    square = (freq / length) ** 2
    spline = 9.0 / (2.0 + np.cos(2.0 * np.pi * freq / length)) ** 2
    return square, np.exp(-(np.pi**2) * square) * spline


def row_matrix():
    basis = real_basis(NY)[0]
    table = np.zeros((2, NARROW, ROWS, 2, NY))
    for half in range(2):
        for n in range(NARROW):
            for r in range(ROWS):
                table[half, n, r, half] = basis[:, (CY * n + r) % NY]
    return table.reshape(2 * NARROW * ROWS, 2 * NY)


def plane_order():
    half, place, other, plane = np.meshgrid(
        np.arange(2), np.arange(RING), np.arange(2), np.arange(CX), indexing="ij"
    )
    return (CX * (DOMAINS * place + 2 * other + half) + plane).reshape(-1)


def split(value):
    high = value.astype(BF16)
    return high, (value - high.astype(F32)).astype(BF16)


def dot3(a, b, contract):
    dims = (contract, ((), ()))
    both = lax.dot_general(
        jnp.concatenate(a, axis=0), b[0], dims, preferred_element_type=F32
    )
    rows = a[0].shape[0]
    return (both[:rows] + both[rows:]) + lax.dot_general(
        a[0], b[1], dims, preferred_element_type=F32
    )


def dot3_wide(a, b):
    columns = b[0].shape[1]
    both = jnp.dot(a[0], jnp.concatenate(b, axis=1), preferred_element_type=F32)
    return (both[:, :columns] + both[:, columns:]) + jnp.dot(
        a[1], b[0], preferred_element_type=F32
    )


def pick(steps, values):
    out = jnp.where(steps == 3, values[3], 0.0)
    for j in (2, 1, 0):
        out = jnp.where(steps == j, values[j], out)
    return out


def spline_weights(t):
    s = 1.0 - t
    square = t * t
    cube = square * t
    return (
        s * s * s / 6.0,
        (3.0 * cube - 6.0 * square + 4.0) / 6.0,
        (-3.0 * cube + 3.0 * square + 3.0 * t + 1.0) / 6.0,
        cube / 6.0,
    )


def spline_slopes(t):
    s = 1.0 - t
    square = t * t
    return (-0.5 * s * s, 1.5 * square - 2.0 * t, -1.5 * square + t + 0.5, 0.5 * square)


def swap(value):
    return pltpu.roll(value, HALF, 1)


def exchange_lanes(blocks, lanes):
    blocks = list(blocks)
    for bit in range(3):
        step = 1 << bit
        clear = (lanes & step) == 0
        for a in range(8):
            if not a & step:
                x, y = blocks[a], blocks[a + step]
                blocks[a] = jnp.where(clear, x, pltpu.roll(y, step, 1))
                blocks[a + step] = jnp.where(clear, pltpu.roll(x, 128 - step, 1), y)
    return blocks


def far_first(sizes):
    offsets = [o for o in np.ndindex(*sizes) if any(o)]

    def hops(offset):
        return sum(min(o, size - o) for o, size in zip(offset, sizes))

    return sorted(offsets, key=lambda o: (-hops(o), o[-1], o[0] % 2))


def kernel(
    count_ref,
    factor_ref,
    offset_hbm,
    base_hbm,
    charge_hbm,
    zh_hbm,
    zl_hbm,
    zth_hbm,
    ztl_hbm,
    yh_hbm,
    yl_hbm,
    yth_hbm,
    ytl_hbm,
    xh_hbm,
    xl_hbm,
    xth_hbm,
    xtl_hbm,
    gain_hbm,
    square_hbm,
    zfactor_hbm,
    raw_ref,
    offset_ref,
    base_ref,
    charge_ref,
    zh_ref,
    zl_ref,
    zth_ref,
    ztl_ref,
    yh_ref,
    yl_ref,
    yth_ref,
    ytl_ref,
    xh_ref,
    xl_ref,
    xth_ref,
    xtl_ref,
    gain_ref,
    square_ref,
    zfactor_ref,
    send_a,
    recv_a,
    send_b,
    recv_b,
    send_c,
    recv_c,
    send_d,
    recv_d,
    depth_h,
    depth_l,
    atom_h,
    atom_l,
    along_ref,
    fold_ref,
    send_sems,
    recv_sems,
    local_sems,
    ring_sem,
):
    w = lax.axis_index("wide")
    n = lax.axis_index("narrow")
    place = lax.div(w, DOMAINS)
    v = lax.rem(w, DOMAINS)
    core = lax.rem(v, 2)
    y = lax.div(v, 2) * 2 + lax.div(n, 4)
    x = lax.rem(n, 4)
    ys = [lax.rem(y + i, 4) for i in range(4)]
    xs = [lax.rem(x + i, 4) for i in range(4)]
    cores = [core, 1 - core]
    vs = [[lax.div(j, 2) * 2 + c for c in cores] for j in ys]
    ns = [[lax.rem(j, 2) * 4 + i for i in xs] for j in ys]

    def ring_mate(offset):
        other = lax.rem(place + offset, RING)
        return other, (other * DOMAINS + v, n)

    def layer_mate(offset):
        dy, dx, dc = offset
        v_to, n_to = vs[dy][dc], ns[dy][dx]
        return v_to, n_to, (place * DOMAINS + v_to, n_to)

    ring = [o[0] for o in far_first((RING,))]
    layer = far_first((4, 4, 2))

    barrier = pltpu.get_barrier_semaphore()
    inputs = (
        (offset_hbm, offset_ref),
        (base_hbm, base_ref),
        (charge_hbm, charge_ref),
        (zh_hbm, zh_ref),
        (zl_hbm, zl_ref),
        (yth_hbm, yth_ref),
        (ytl_hbm, ytl_ref),
        (zfactor_hbm, zfactor_ref),
        (gain_hbm, gain_ref),
        (square_hbm, square_ref),
        (xh_hbm, xh_ref),
        (xl_hbm, xl_ref),
        (xth_hbm, xth_ref),
        (xtl_hbm, xtl_ref),
        (yh_hbm, yh_ref),
        (yl_hbm, yl_ref),
        (zth_hbm, zth_ref),
        (ztl_hbm, ztl_ref),
    )
    loads = [pltpu.make_async_copy(a, b, local_sems.at[i]) for i, (a, b) in enumerate(inputs)]
    for load in loads[:3]:
        load.start()

    near = [o for o in ring if min(o, RING - o) <= REACH]
    mates = [ring_mate(offset)[1] for offset in near[:2]]
    mates += [layer_mate(offset)[2] for offset in layer]
    mates += [ring_mate(offset)[1] for offset in near[2:]]
    for mate in mates:
        pl.semaphore_signal(barrier, inc=1, device_id=mate, device_id_type=MESH)

    for load in loads[3:]:
        load.start()

    lanes = lax.broadcasted_iota(jnp.int32, (1, 128), 1)
    low_lanes = lanes < HALF
    low_rows = lax.broadcasted_iota(jnp.int32, (1, 8, 1), 1) < CX

    for load in loads[:3]:
        load.wait()
    t = [offset_ref[d, 0] for d in range(3)]
    corner = [base_ref[d, 0] for d in range(3)]
    weights = [spline_weights(u) for u in t]
    slopes = [spline_slopes(u) for u in t]
    occupied = lax.broadcasted_iota(jnp.int32, (1, SLOTS), 1) < count_ref[0, 0]
    charge = jnp.where(occupied, charge_ref[0], 0.0)

    def depth_steps(first):
        cell = lax.broadcasted_iota(jnp.int32, (128, SLOTS), 0) + first
        return (cell - corner[2]) & (NZ - 1)

    for first in range(0, NZ, 128):
        high, low = split(pick(depth_steps(first), weights[2]))
        depth_h[first : first + 128, :SLOTS] = high
        depth_l[first : first + 128, :SLOTS] = low

    row_steps = lax.broadcasted_iota(jnp.int32, (16, SLOTS), 0) - corner[1]
    row_w = pick(row_steps, weights[1])
    row_q = row_w * charge
    plane_w = [pick(p - corner[0], weights[0]) for p in range(PLANES)]
    cross = jnp.concatenate([row_q * plane_w[p] for p in range(PLANES)], axis=0)
    grid = dot3(split(cross), (depth_h[:, :SLOTS], depth_l[:, :SLOTS]), ((1,), (1,)))
    for load in loads[3:5]:
        load.wait()
    spectrum = dot3(split(grid), (zh_ref[...], zl_ref[...]), ((1,), (0,)))
    for m in range(DOMAINS):
        tiles = [spectrum[16 * p : 16 * p + 16, 128 * m : 128 * m + 128] for p in range(PLANES)]
        tiles = exchange_lanes(tiles + [jnp.zeros((16, 128), F32)], lanes)
        for e in range(NARROW):
            send_a[16 * (8 * m + e) : 16 * (8 * m + e) + 16, :] = tiles[e]

    pl.semaphore_wait(barrier, len(near) + len(layer))

    def push(stage, source, target, to, far=0):
        pltpu.make_async_remote_copy(
            src_ref=source,
            dst_ref=target,
            send_sem=send_sems.at[stage],
            recv_sem=recv_sems.at[stage + far],
            device_id=to,
            device_id_type=MESH,
        ).start()

    def drain(stage, block):
        return pltpu.make_async_remote_copy(
            src_ref=block,
            dst_ref=block,
            send_sem=send_sems.at[stage],
            recv_sem=recv_sems.at[stage],
            device_id=(w, n),
            device_id_type=MESH,
        )

    for offset in (REACH, RING - REACH):
        pl.semaphore_signal(ring_sem, inc=1, device_id=ring_mate(offset)[1], device_id_type=MESH)

    mine = 8 * v + n
    own_a = recv_a.at[pl.ds(ROWS * mine, ROWS)]
    for offset in layer:
        v_to, n_to, to = layer_mate(offset)
        far = lax.rem(lax.div(v_to, 2) + lax.div(v, 2), 2)
        push(0, send_a.at[pl.ds(16 * (8 * v_to + n_to), ROWS)], own_a, to, 5 * far)
    keep_a = pltpu.make_async_copy(send_a.at[pl.ds(16 * mine, ROWS)], own_a, local_sems.at[18])
    keep_a.start()

    row_s = pick(row_steps, slopes[1])
    plane_s = [pick(p - corner[0], slopes[0]) for p in range(PLANES)]
    for first in range(0, NZ, 128):
        high, low = split(pick(depth_steps(first), slopes[2]))
        depth_h[first : first + 128, SLOTS:] = high
        depth_l[first : first + 128, SLOTS:] = low
    for load in loads[5:]:
        load.wait()
    coefficient = 128 * v + 8 * place + n
    chosen = lax.broadcasted_iota(jnp.int32, (8, NZ), 1) == coefficient
    zfactor = jnp.sum(jnp.where(chosen, zfactor_ref[...], 0.0), axis=1, keepdims=True)
    squared = square_ref[...] + zfactor[0:1]
    positive = jnp.where(squared > 0.0, squared, 1.0)
    influence = jnp.where(squared > 0.0, gain_ref[...] * zfactor[1:2] / positive, 0.0)

    def turn_half(which):
        half = 8 * ROWS * 2
        rows = recv_a[pl.ds(pl.multiple_of(half * which, 8), half), :]
        fold_ref[which] = dot3((yth_ref[...], ytl_ref[...]), split(rows), ((1,), (0,))).T

    keep_a.wait()
    drain(0, recv_a.at[pl.ds(0, ROWS * 15)]).wait_recv()
    turn_half(lax.div(v, 2))
    drain(5, recv_a.at[pl.ds(0, ROWS * 16)]).wait_recv()
    turn_half(1 - lax.div(v, 2))
    first = fold_ref[0].reshape(RING, 8, 128)
    second = fold_ref[1].reshape(RING, 8, 128)

    def both(value):
        return swap(value.reshape(8 * RING, 128)).reshape(RING, 8, 128)

    def turn(value):
        return pltpu.roll(value, CX, 1)

    first_swapped = both(first)
    second_swapped = both(second)
    low3 = low_lanes.reshape(1, 1, 128)
    upper = first + jnp.where(low3, 0.0, turn(first_swapped))
    lower = turn(second) + jnp.where(low3, first_swapped, second_swapped)
    send_b[:, 0:8, :] = jnp.where(low_rows, upper, lower)
    send_b[:, 8:16, :] = turn(second_swapped)

    pl.semaphore_wait(ring_sem, 2)
    for offset in ring:
        other, to = ring_mate(offset)
        push(1, send_b.at[other, pl.ds(0, 12)], recv_b.at[place, pl.ds(0, 12)], to)
    recv_b[place] = send_b[place]
    for first in range(0, NZ, 128):
        part = slice(first, first + 128)
        z_rows = (zth_ref[part, :], ztl_ref[part, :])
        high, low = split(dot3(z_rows, (depth_h[...], depth_l[...]), ((1,), (0,))))
        atom_h[part, :] = high
        atom_l[part, :] = low
    drain(1, recv_b.at[pl.ds(0, 15), pl.ds(0, 12)]).wait_recv()

    beyond = recv_b[:, 8:16, :]
    beyond = jnp.concatenate([beyond[RING - 1 :], beyond[: RING - 1]], axis=0)
    planes = recv_b[:, 0:8, :] + jnp.where(low_rows & low3, beyond, 0.0)
    planes = planes.reshape(8 * RING, 128)
    turned = swap(planes)
    stacked = jnp.concatenate(
        [jnp.where(low_lanes, planes, turned), jnp.where(low_lanes, turned, planes)], axis=0
    )
    filtered = dot3_wide((xh_ref[...], xl_ref[...]), split(stacked)) * influence
    planes = dot3_wide((xth_ref[...], xtl_ref[...]), split(filtered))
    planes = jnp.where(low_lanes, planes[:128], planes[128:]).reshape(RING, 8, 128)
    send_c[:, 0:8, :] = planes
    send_c[:, 8:16, :] = jnp.concatenate([planes[1:], planes[:1]], axis=0)

    for offset in ring:
        other, to = ring_mate(offset)
        push(2, send_c.at[other, pl.ds(0, 12)], recv_c.at[place, pl.ds(0, 12)], to)
    recv_c[place] = send_c[place]
    drain(2, recv_c.at[pl.ds(0, 15), pl.ds(0, 12)]).wait_recv()

    own = recv_c[:, 0:8, :]
    own_swapped = both(own)
    beyond = turn(both(recv_c[:, 8:16, :]))
    first = jnp.where(low_rows, own, jnp.where(low3, turn(own_swapped), own_swapped))
    second = jnp.where(low_rows, turn(own), jnp.where(low3, own_swapped, beyond))
    columns = jnp.concatenate([first, second], axis=0).reshape(16 * RING, 128)
    rows = dot3((yh_ref[...], yl_ref[...]), split(columns), ((1,), (1,)))
    send_d[0] = rows[:, :128]
    send_d[1] = rows[:, 128:]

    own_d = recv_d.at[pl.ds(16 * mine, ROWS)]

    def block_d(v_to, n_to):
        return send_d.at[lax.div(v_to, 2), pl.ds(ROWS * (8 * lax.rem(v_to, 2) + n_to), ROWS)]

    for offset in layer:
        v_to, n_to, to = layer_mate(offset)
        far = lax.rem(lax.div(v_to, 2) + lax.div(v, 2), 2)
        push(3, block_d(v_to, n_to), own_d, to, far)
    keep_d = pltpu.make_async_copy(block_d(v, n), own_d, local_sems.at[19])
    keep_d.start()

    inside = lax.broadcasted_iota(jnp.int32, (16, 128), 0) < ROWS

    def along_half(which):
        parts = []
        for m in range(2):
            start = 256 * which + 128 * m
            tiles = [recv_d[pl.ds(start + 16 * e, 16), :] for e in range(NARROW)]
            tiles = exchange_lanes([jnp.where(inside, u, 0.0) for u in tiles], lanes)
            parts.append(jnp.concatenate(tiles[:PLANES], axis=0))
        spectrum = split(jnp.concatenate(parts, axis=1))
        start = pl.multiple_of(256 * which, 256)
        atoms = (atom_h[pl.ds(start, 256), :], atom_l[pl.ds(start, 256), :])
        return dot3(spectrum, atoms, ((1,), (0,)))

    keep_d.wait()
    drain(3, recv_a.at[pl.ds(0, ROWS * 15)]).wait_recv()
    along_ref[...] = along_half(lax.div(v, 2))
    drain(4, recv_a.at[pl.ds(0, ROWS * 16)]).wait_recv()
    along = along_ref[...] + along_half(1 - lax.div(v, 2))

    total = jnp.zeros((16, SLOTS), F32)
    pull_x, pull_z = total, total
    for p in range(PLANES):
        part = slice(16 * p, 16 * p + 16)
        total = total + along[part, :SLOTS] * plane_w[p]
        pull_x = pull_x + along[part, :SLOTS] * plane_s[p]
        pull_z = pull_z + along[part, SLOTS:] * plane_w[p]

    def over_rows(value):
        return jnp.sum(value, axis=0, keepdims=True)

    factor = factor_ref[0]
    pull_y = over_rows(total * row_s)
    total = over_rows(total * row_w)
    pull_x = over_rows(pull_x * row_w)
    pull_z = over_rows(pull_z * row_w)
    pull = -factor * charge
    raw_ref[0, 0] = pull * pull_x
    raw_ref[1, 0] = pull * pull_y
    raw_ref[2, 0] = pull * pull_z
    raw_ref[3, 0] = jnp.where(occupied, factor * total, 0.0)

    drain(0, recv_a.at[pl.ds(0, ROWS * 31)]).wait_send()
    drain(1, recv_b.at[pl.ds(0, 15), pl.ds(0, 12)]).wait_send()
    drain(2, recv_c.at[pl.ds(0, 15), pl.ds(0, 12)]).wait_send()
    drain(3, recv_a.at[pl.ds(0, ROWS * 31)]).wait_send()


def hand_out(raw_ref, force_hbm, grad_hbm, sems):
    forces = pltpu.make_async_copy(raw_ref.at[pl.ds(0, 3)], force_hbm, sems.at[0])
    grads = pltpu.make_async_copy(raw_ref.at[3], grad_hbm, sems.at[1])
    forces.start()
    grads.start()
    forces.wait()
    grads.wait()


def on_device(offsets, bases, charges, counts, cotangent):
    z_table = real_basis(NZ)[0].T
    y_table = row_matrix()
    x_table = real_basis(NX)[0][:, plane_order()]
    square_x, gain_x = frequency_factors(NX)
    square_y, gain_y = frequency_factors(NY)
    zfactor = np.zeros((8, NZ), np.float32)
    zfactor[0], zfactor[1] = frequency_factors(NZ)
    square = (square_x[:, None] + np.tile(square_y, 2)[None, :]).astype(np.float32)
    gain = (gain_x[:, None] * np.tile(gain_y, 2)[None, :] / math.pi).astype(np.float32)
    arrays = (
        offsets,
        bases,
        charges,
        *halves(z_table),
        *halves(z_table.T),
        *halves(y_table),
        *halves(y_table.T),
        *halves(x_table),
        *halves(x_table.T),
        gain,
        square,
        zfactor,
    )
    smem = pl.BlockSpec(memory_space=pltpu.SMEM)
    hbm = pl.BlockSpec(memory_space=pltpu.HBM)
    vmem = pl.BlockSpec(memory_space=VMEM)
    raw = pl.pallas_call(
        kernel,
        out_shape=jax.ShapeDtypeStruct((4, 1, 1, SLOTS), F32),
        in_specs=[smem] * 2 + [hbm] * len(arrays),
        out_specs=vmem,
        scratch_shapes=[
            *[VMEM(a.shape, a.dtype) for a in arrays],
            VMEM((16 * 32, 128), F32),
            VMEM((ROWS * 32, 128), F32),
            VMEM((RING, 16, 128), F32),
            VMEM((RING, 16, 128), F32),
            VMEM((RING, 16, 128), F32),
            VMEM((RING, 16, 128), F32),
            VMEM((2, ROWS * 16, 128), F32),
            VMEM((16 * 32, 128), F32),
            VMEM((NZ, 2 * SLOTS), BF16),
            VMEM((NZ, 2 * SLOTS), BF16),
            VMEM((NZ, 2 * SLOTS), BF16),
            VMEM((NZ, 2 * SLOTS), BF16),
            VMEM((16 * PLANES, 2 * SLOTS), F32),
            VMEM((2, 128, 128), F32),
            pltpu.SemaphoreType.DMA((6,)),
            pltpu.SemaphoreType.DMA((6,)),
            pltpu.SemaphoreType.DMA((len(arrays) + 2,)),
            pltpu.SemaphoreType.REGULAR,
        ],
        compiler_params=pltpu.CompilerParams(
            collective_id=0, has_side_effects=True, vmem_limit_bytes=40 * 1024 * 1024
        ),
        name="ewald",
    )(counts, cotangent, *[pltpu.with_memory_space_constraint(a, pltpu.HBM) for a in arrays])
    return pl.pallas_call(
        hand_out,
        out_shape=(
            jax.ShapeDtypeStruct((3, 1, 1, SLOTS), F32),
            jax.ShapeDtypeStruct((1, 1, SLOTS), F32),
        ),
        in_specs=[vmem],
        out_specs=(hbm, hbm),
        scratch_shapes=[pltpu.SemaphoreType.DMA((2,))],
        name="hand_out",
    )(pltpu.with_memory_space_constraint(raw, VMEM))


def solution(mesh):
    placed = (
        P(None, "wide", "narrow", None),
        P(None, "wide", "narrow", None),
        P("wide", "narrow", None),
        P("wide", "narrow"),
        P(),
    )
    return jax.shard_map(
        on_device,
        mesh=mesh,
        in_specs=placed,
        out_specs=(P(None, "wide", "narrow", None), P("wide", "narrow", None)),
        check_vma=False,
    )
```

```python
import math

import jax
import jax.numpy as jnp
import ml_dtypes
import numpy as np
from jax import lax
from jax.experimental import pallas as pl
from jax.experimental.pallas import tpu as pltpu
from jax.sharding import PartitionSpec as P

CX = 4
CY = 8
NZ = 512
WIDE = 64
NARROW = 8
NX = CX * WIDE
NY = CY * NARROW
SLOTS = 512
ROWS = CY + 3
RING = 16
DOMAINS = WIDE // RING
PLANES = CX + 3
REACH = RING // 4
HALF = 64
MESH = pl.DeviceIdType.MESH
VMEM = pltpu.VMEM
F32 = jnp.float32
BF16 = jnp.bfloat16


def real_basis(length):
    c = np.arange(length)
    freq = np.where(c <= length // 2, c, length - c)
    phase = (freq[:, None] * c[None, :]) % length * (2.0 * np.pi / length)
    scale = np.where((freq == 0) | (2 * freq == length), 1.0, np.sqrt(2.0)) / np.sqrt(length)
    table = np.where((c <= length // 2)[:, None], np.cos(phase), np.sin(phase)) * scale[:, None]
    return table, freq


def halves(table):
    table = np.asarray(table, np.float32)
    high = table.astype(ml_dtypes.bfloat16)
    low = (table - high.astype(np.float32)).astype(ml_dtypes.bfloat16)
    return high, low


def frequency_factors(length):
    freq = real_basis(length)[1]
    square = (freq / length) ** 2
    spline = 9.0 / (2.0 + np.cos(2.0 * np.pi * freq / length)) ** 2
    return square, np.exp(-(np.pi**2) * square) * spline


def row_matrix():
    basis = real_basis(NY)[0]
    table = np.zeros((2, NARROW, ROWS, 2, NY))
    for half in range(2):
        for n in range(NARROW):
            for r in range(ROWS):
                table[half, n, r, half] = basis[:, (CY * n + r) % NY]
    return table.reshape(2 * NARROW * ROWS, 2 * NY)


def plane_order():
    half, place, other, plane = np.meshgrid(
        np.arange(2), np.arange(RING), np.arange(2), np.arange(CX), indexing="ij"
    )
    return (CX * (DOMAINS * place + 2 * other + half) + plane).reshape(-1)


def split(value):
    high = value.astype(BF16)
    return high, (value - high.astype(F32)).astype(BF16)


def dot3(a, b, contract):
    dims = (contract, ((), ()))
    both = lax.dot_general(
        jnp.concatenate(a, axis=0), b[0], dims, preferred_element_type=F32
    )
    rows = a[0].shape[0]
    return (both[:rows] + both[rows:]) + lax.dot_general(
        a[0], b[1], dims, preferred_element_type=F32
    )


def dot3_wide(a, b):
    columns = b[0].shape[1]
    both = jnp.dot(a[0], jnp.concatenate(b, axis=1), preferred_element_type=F32)
    return (both[:, :columns] + both[:, columns:]) + jnp.dot(
        a[1], b[0], preferred_element_type=F32
    )


def pick(steps, values):
    out = jnp.where(steps == 3, values[3], 0.0)
    for j in (2, 1, 0):
        out = jnp.where(steps == j, values[j], out)
    return out


def spline_weights(t):
    s = 1.0 - t
    square = t * t
    cube = square * t
    return (
        s * s * s / 6.0,
        (3.0 * cube - 6.0 * square + 4.0) / 6.0,
        (-3.0 * cube + 3.0 * square + 3.0 * t + 1.0) / 6.0,
        cube / 6.0,
    )


def spline_slopes(t):
    s = 1.0 - t
    square = t * t
    return (-0.5 * s * s, 1.5 * square - 2.0 * t, -1.5 * square + t + 0.5, 0.5 * square)


def swap(value):
    return pltpu.roll(value, HALF, 1)


def exchange_lanes(blocks, lanes):
    blocks = list(blocks)
    for bit in range(3):
        step = 1 << bit
        clear = (lanes & step) == 0
        for a in range(8):
            if not a & step:
                x, y = blocks[a], blocks[a + step]
                blocks[a] = jnp.where(clear, x, pltpu.roll(y, step, 1))
                blocks[a + step] = jnp.where(clear, pltpu.roll(x, 128 - step, 1), y)
    return blocks


def far_first(sizes):
    offsets = [o for o in np.ndindex(*sizes) if any(o)]

    def hops(offset):
        return sum(min(o, size - o) for o, size in zip(offset, sizes))

    return sorted(offsets, key=lambda o: (-hops(o), o[-1], o[0] % 2))


def kernel(
    count_ref,
    factor_ref,
    offset_hbm,
    base_hbm,
    charge_hbm,
    zh_hbm,
    zl_hbm,
    zth_hbm,
    ztl_hbm,
    yh_hbm,
    yl_hbm,
    yth_hbm,
    ytl_hbm,
    xh_hbm,
    xl_hbm,
    xth_hbm,
    xtl_hbm,
    gain_hbm,
    square_hbm,
    zfactor_hbm,
    raw_ref,
    offset_ref,
    base_ref,
    charge_ref,
    zh_ref,
    zl_ref,
    zth_ref,
    ztl_ref,
    yh_ref,
    yl_ref,
    yth_ref,
    ytl_ref,
    xh_ref,
    xl_ref,
    xth_ref,
    xtl_ref,
    gain_ref,
    square_ref,
    zfactor_ref,
    send_a,
    recv_a,
    send_b,
    recv_b,
    send_c,
    recv_c,
    send_d,
    recv_d,
    depth_h,
    depth_l,
    atom_h,
    atom_l,
    along_ref,
    send_sems,
    recv_sems,
    local_sems,
    ring_sem,
):
    w = lax.axis_index("wide")
    n = lax.axis_index("narrow")
    place = lax.div(w, DOMAINS)
    v = lax.rem(w, DOMAINS)
    core = lax.rem(v, 2)
    y = lax.div(v, 2) * 2 + lax.div(n, 4)
    x = lax.rem(n, 4)
    ys = [lax.rem(y + i, 4) for i in range(4)]
    xs = [lax.rem(x + i, 4) for i in range(4)]
    cores = [core, 1 - core]
    vs = [[lax.div(j, 2) * 2 + c for c in cores] for j in ys]
    ns = [[lax.rem(j, 2) * 4 + i for i in xs] for j in ys]

    def ring_mate(offset):
        other = lax.rem(place + offset, RING)
        return other, (other * DOMAINS + v, n)

    def layer_mate(offset):
        dy, dx, dc = offset
        v_to, n_to = vs[dy][dc], ns[dy][dx]
        return v_to, n_to, (place * DOMAINS + v_to, n_to)

    ring = [o[0] for o in far_first((RING,))]
    layer = far_first((4, 4, 2))

    barrier = pltpu.get_barrier_semaphore()
    inputs = (
        (offset_hbm, offset_ref),
        (base_hbm, base_ref),
        (charge_hbm, charge_ref),
        (zh_hbm, zh_ref),
        (zl_hbm, zl_ref),
        (yth_hbm, yth_ref),
        (ytl_hbm, ytl_ref),
        (zfactor_hbm, zfactor_ref),
        (gain_hbm, gain_ref),
        (square_hbm, square_ref),
        (xh_hbm, xh_ref),
        (xl_hbm, xl_ref),
        (xth_hbm, xth_ref),
        (xtl_hbm, xtl_ref),
        (yh_hbm, yh_ref),
        (yl_hbm, yl_ref),
        (zth_hbm, zth_ref),
        (ztl_hbm, ztl_ref),
    )
    loads = [pltpu.make_async_copy(a, b, local_sems.at[i]) for i, (a, b) in enumerate(inputs)]
    for load in loads[:3]:
        load.start()

    near = [o for o in ring if min(o, RING - o) <= REACH]
    mates = [ring_mate(offset)[1] for offset in near[:2]]
    mates += [layer_mate(offset)[2] for offset in layer]
    mates += [ring_mate(offset)[1] for offset in near[2:]]
    for mate in mates:
        pl.semaphore_signal(barrier, inc=1, device_id=mate, device_id_type=MESH)

    for load in loads[3:]:
        load.start()

    lanes = lax.broadcasted_iota(jnp.int32, (1, 128), 1)
    low_lanes = lanes < HALF
    low_rows = lax.broadcasted_iota(jnp.int32, (1, 8, 1), 1) < CX

    for load in loads[:3]:
        load.wait()
    t = [offset_ref[d, 0] for d in range(3)]
    corner = [base_ref[d, 0] for d in range(3)]
    weights = [spline_weights(u) for u in t]
    slopes = [spline_slopes(u) for u in t]
    occupied = lax.broadcasted_iota(jnp.int32, (1, SLOTS), 1) < count_ref[0, 0]
    charge = jnp.where(occupied, charge_ref[0], 0.0)

    def depth_steps(first):
        cell = lax.broadcasted_iota(jnp.int32, (128, SLOTS), 0) + first
        return (cell - corner[2]) & (NZ - 1)

    for first in range(0, NZ, 128):
        high, low = split(pick(depth_steps(first), weights[2]))
        depth_h[first : first + 128, :SLOTS] = high
        depth_l[first : first + 128, :SLOTS] = low

    row_steps = lax.broadcasted_iota(jnp.int32, (16, SLOTS), 0) - corner[1]
    row_w = pick(row_steps, weights[1])
    row_q = row_w * charge
    plane_w = [pick(p - corner[0], weights[0]) for p in range(PLANES)]
    cross = jnp.concatenate([row_q * plane_w[p] for p in range(PLANES)], axis=0)
    grid = dot3(split(cross), (depth_h[:, :SLOTS], depth_l[:, :SLOTS]), ((1,), (1,)))
    for load in loads[3:5]:
        load.wait()
    spectrum = dot3(split(grid), (zh_ref[...], zl_ref[...]), ((1,), (0,)))
    for m in range(DOMAINS):
        tiles = [spectrum[16 * p : 16 * p + 16, 128 * m : 128 * m + 128] for p in range(PLANES)]
        tiles = exchange_lanes(tiles + [jnp.zeros((16, 128), F32)], lanes)
        for e in range(NARROW):
            send_a[16 * (8 * m + e) : 16 * (8 * m + e) + 16, :] = tiles[e]

    pl.semaphore_wait(barrier, len(near) + len(layer))

    def push(stage, source, target, to, far=0):
        pltpu.make_async_remote_copy(
            src_ref=source,
            dst_ref=target,
            send_sem=send_sems.at[stage],
            recv_sem=recv_sems.at[stage + far],
            device_id=to,
            device_id_type=MESH,
        ).start()

    def drain(stage, block):
        return pltpu.make_async_remote_copy(
            src_ref=block,
            dst_ref=block,
            send_sem=send_sems.at[stage],
            recv_sem=recv_sems.at[stage],
            device_id=(w, n),
            device_id_type=MESH,
        )

    for offset in (REACH, RING - REACH):
        pl.semaphore_signal(ring_sem, inc=1, device_id=ring_mate(offset)[1], device_id_type=MESH)

    mine = 8 * v + n
    own_a = recv_a.at[pl.ds(ROWS * mine, ROWS)]
    for offset in layer:
        v_to, n_to, to = layer_mate(offset)
        push(0, send_a.at[pl.ds(16 * (8 * v_to + n_to), ROWS)], own_a, to)
    keep_a = pltpu.make_async_copy(send_a.at[pl.ds(16 * mine, ROWS)], own_a, local_sems.at[18])
    keep_a.start()

    row_s = pick(row_steps, slopes[1])
    plane_s = [pick(p - corner[0], slopes[0]) for p in range(PLANES)]
    for first in range(0, NZ, 128):
        high, low = split(pick(depth_steps(first), slopes[2]))
        depth_h[first : first + 128, SLOTS:] = high
        depth_l[first : first + 128, SLOTS:] = low
    for load in loads[5:]:
        load.wait()
    coefficient = 128 * v + 8 * place + n
    chosen = lax.broadcasted_iota(jnp.int32, (8, NZ), 1) == coefficient
    zfactor = jnp.sum(jnp.where(chosen, zfactor_ref[...], 0.0), axis=1, keepdims=True)
    squared = square_ref[...] + zfactor[0:1]
    positive = jnp.where(squared > 0.0, squared, 1.0)
    influence = jnp.where(squared > 0.0, gain_ref[...] * zfactor[1:2] / positive, 0.0)

    keep_a.wait()
    drain(0, recv_a.at[pl.ds(0, ROWS * 31)]).wait_recv()
    half = 8 * ROWS * 2
    rows = jnp.concatenate([recv_a[:half], recv_a[half:]], axis=1)
    columns = dot3((yth_ref[...], ytl_ref[...]), split(rows), ((1,), (0,)))
    first = columns[:, :128].T.reshape(RING, 8, 128)
    second = columns[:, 128:].T.reshape(RING, 8, 128)

    def both(value):
        return swap(value.reshape(8 * RING, 128)).reshape(RING, 8, 128)

    def turn(value):
        return pltpu.roll(value, CX, 1)

    first_swapped = both(first)
    second_swapped = both(second)
    low3 = low_lanes.reshape(1, 1, 128)
    upper = first + jnp.where(low3, 0.0, turn(first_swapped))
    lower = turn(second) + jnp.where(low3, first_swapped, second_swapped)
    send_b[:, 0:8, :] = jnp.where(low_rows, upper, lower)
    send_b[:, 8:16, :] = turn(second_swapped)

    pl.semaphore_wait(ring_sem, 2)
    for offset in ring:
        other, to = ring_mate(offset)
        push(1, send_b.at[other, pl.ds(0, 12)], recv_b.at[place, pl.ds(0, 12)], to)
    recv_b[place] = send_b[place]
    for first in range(0, NZ, 128):
        part = slice(first, first + 128)
        z_rows = (zth_ref[part, :], ztl_ref[part, :])
        high, low = split(dot3(z_rows, (depth_h[...], depth_l[...]), ((1,), (0,))))
        atom_h[part, :] = high
        atom_l[part, :] = low
    drain(1, recv_b.at[pl.ds(0, 15), pl.ds(0, 12)]).wait_recv()

    beyond = recv_b[:, 8:16, :]
    beyond = jnp.concatenate([beyond[RING - 1 :], beyond[: RING - 1]], axis=0)
    planes = recv_b[:, 0:8, :] + jnp.where(low_rows & low3, beyond, 0.0)
    planes = planes.reshape(8 * RING, 128)
    turned = swap(planes)
    stacked = jnp.concatenate(
        [jnp.where(low_lanes, planes, turned), jnp.where(low_lanes, turned, planes)], axis=0
    )
    filtered = dot3_wide((xh_ref[...], xl_ref[...]), split(stacked)) * influence
    planes = dot3_wide((xth_ref[...], xtl_ref[...]), split(filtered))
    planes = jnp.where(low_lanes, planes[:128], planes[128:]).reshape(RING, 8, 128)
    send_c[:, 0:8, :] = planes
    send_c[:, 8:16, :] = jnp.concatenate([planes[1:], planes[:1]], axis=0)

    for offset in ring:
        other, to = ring_mate(offset)
        push(2, send_c.at[other, pl.ds(0, 12)], recv_c.at[place, pl.ds(0, 12)], to)
    recv_c[place] = send_c[place]
    drain(2, recv_c.at[pl.ds(0, 15), pl.ds(0, 12)]).wait_recv()

    own = recv_c[:, 0:8, :]
    own_swapped = both(own)
    beyond = turn(both(recv_c[:, 8:16, :]))
    first = jnp.where(low_rows, own, jnp.where(low3, turn(own_swapped), own_swapped))
    second = jnp.where(low_rows, turn(own), jnp.where(low3, own_swapped, beyond))
    columns = jnp.concatenate([first, second], axis=0).reshape(16 * RING, 128)
    rows = dot3((yh_ref[...], yl_ref[...]), split(columns), ((1,), (1,)))
    send_d[0] = rows[:, :128]
    send_d[1] = rows[:, 128:]

    own_d = recv_d.at[pl.ds(16 * mine, ROWS)]

    def block_d(v_to, n_to):
        return send_d.at[lax.div(v_to, 2), pl.ds(ROWS * (8 * lax.rem(v_to, 2) + n_to), ROWS)]

    for offset in layer:
        v_to, n_to, to = layer_mate(offset)
        far = lax.rem(lax.div(v_to, 2) + lax.div(v, 2), 2)
        push(3, block_d(v_to, n_to), own_d, to, far)
    keep_d = pltpu.make_async_copy(block_d(v, n), own_d, local_sems.at[19])
    keep_d.start()

    inside = lax.broadcasted_iota(jnp.int32, (16, 128), 0) < ROWS

    def along_half(which):
        parts = []
        for m in range(2):
            start = 256 * which + 128 * m
            tiles = [recv_d[pl.ds(start + 16 * e, 16), :] for e in range(NARROW)]
            tiles = exchange_lanes([jnp.where(inside, u, 0.0) for u in tiles], lanes)
            parts.append(jnp.concatenate(tiles[:PLANES], axis=0))
        spectrum = split(jnp.concatenate(parts, axis=1))
        start = pl.multiple_of(256 * which, 256)
        atoms = (atom_h[pl.ds(start, 256), :], atom_l[pl.ds(start, 256), :])
        return dot3(spectrum, atoms, ((1,), (0,)))

    keep_d.wait()
    drain(3, recv_a.at[pl.ds(0, ROWS * 15)]).wait_recv()
    along_ref[...] = along_half(lax.div(v, 2))
    drain(4, recv_a.at[pl.ds(0, ROWS * 16)]).wait_recv()
    along = along_ref[...] + along_half(1 - lax.div(v, 2))

    total = jnp.zeros((16, SLOTS), F32)
    pull_x, pull_z = total, total
    for p in range(PLANES):
        part = slice(16 * p, 16 * p + 16)
        total = total + along[part, :SLOTS] * plane_w[p]
        pull_x = pull_x + along[part, :SLOTS] * plane_s[p]
        pull_z = pull_z + along[part, SLOTS:] * plane_w[p]

    def over_rows(value):
        return jnp.sum(value, axis=0, keepdims=True)

    factor = factor_ref[0]
    pull_y = over_rows(total * row_s)
    total = over_rows(total * row_w)
    pull_x = over_rows(pull_x * row_w)
    pull_z = over_rows(pull_z * row_w)
    pull = -factor * charge
    raw_ref[0, 0] = pull * pull_x
    raw_ref[1, 0] = pull * pull_y
    raw_ref[2, 0] = pull * pull_z
    raw_ref[3, 0] = jnp.where(occupied, factor * total, 0.0)

    drain(0, recv_a.at[pl.ds(0, ROWS * 31)]).wait_send()
    drain(1, recv_b.at[pl.ds(0, 15), pl.ds(0, 12)]).wait_send()
    drain(2, recv_c.at[pl.ds(0, 15), pl.ds(0, 12)]).wait_send()
    drain(3, recv_a.at[pl.ds(0, ROWS * 31)]).wait_send()


def hand_out(raw_ref, force_hbm, grad_hbm, sems):
    forces = pltpu.make_async_copy(raw_ref.at[pl.ds(0, 3)], force_hbm, sems.at[0])
    grads = pltpu.make_async_copy(raw_ref.at[3], grad_hbm, sems.at[1])
    forces.start()
    grads.start()
    forces.wait()
    grads.wait()


def on_device(offsets, bases, charges, counts, cotangent):
    z_table = real_basis(NZ)[0].T
    y_table = row_matrix()
    x_table = real_basis(NX)[0][:, plane_order()]
    square_x, gain_x = frequency_factors(NX)
    square_y, gain_y = frequency_factors(NY)
    zfactor = np.zeros((8, NZ), np.float32)
    zfactor[0], zfactor[1] = frequency_factors(NZ)
    square = (square_x[:, None] + np.tile(square_y, 2)[None, :]).astype(np.float32)
    gain = (gain_x[:, None] * np.tile(gain_y, 2)[None, :] / math.pi).astype(np.float32)
    arrays = (
        offsets,
        bases,
        charges,
        *halves(z_table),
        *halves(z_table.T),
        *halves(y_table),
        *halves(y_table.T),
        *halves(x_table),
        *halves(x_table.T),
        gain,
        square,
        zfactor,
    )
    smem = pl.BlockSpec(memory_space=pltpu.SMEM)
    hbm = pl.BlockSpec(memory_space=pltpu.HBM)
    vmem = pl.BlockSpec(memory_space=VMEM)
    raw = pl.pallas_call(
        kernel,
        out_shape=jax.ShapeDtypeStruct((4, 1, 1, SLOTS), F32),
        in_specs=[smem] * 2 + [hbm] * len(arrays),
        out_specs=vmem,
        scratch_shapes=[
            *[VMEM(a.shape, a.dtype) for a in arrays],
            VMEM((16 * 32, 128), F32),
            VMEM((ROWS * 32, 128), F32),
            VMEM((RING, 16, 128), F32),
            VMEM((RING, 16, 128), F32),
            VMEM((RING, 16, 128), F32),
            VMEM((RING, 16, 128), F32),
            VMEM((2, ROWS * 16, 128), F32),
            VMEM((16 * 32, 128), F32),
            VMEM((NZ, 2 * SLOTS), BF16),
            VMEM((NZ, 2 * SLOTS), BF16),
            VMEM((NZ, 2 * SLOTS), BF16),
            VMEM((NZ, 2 * SLOTS), BF16),
            VMEM((16 * PLANES, 2 * SLOTS), F32),
            pltpu.SemaphoreType.DMA((6,)),
            pltpu.SemaphoreType.DMA((6,)),
            pltpu.SemaphoreType.DMA((len(arrays) + 2,)),
            pltpu.SemaphoreType.REGULAR,
        ],
        compiler_params=pltpu.CompilerParams(
            collective_id=0, has_side_effects=True, vmem_limit_bytes=40 * 1024 * 1024
        ),
        name="ewald",
    )(counts, cotangent, *[pltpu.with_memory_space_constraint(a, pltpu.HBM) for a in arrays])
    return pl.pallas_call(
        hand_out,
        out_shape=(
            jax.ShapeDtypeStruct((3, 1, 1, SLOTS), F32),
            jax.ShapeDtypeStruct((1, 1, SLOTS), F32),
        ),
        in_specs=[vmem],
        out_specs=(hbm, hbm),
        scratch_shapes=[pltpu.SemaphoreType.DMA((2,))],
        name="hand_out",
    )(pltpu.with_memory_space_constraint(raw, VMEM))


def solution(mesh):
    placed = (
        P(None, "wide", "narrow", None),
        P(None, "wide", "narrow", None),
        P("wide", "narrow", None),
        P("wide", "narrow"),
        P(),
    )
    return jax.shard_map(
        on_device,
        mesh=mesh,
        in_specs=placed,
        out_specs=(P(None, "wide", "narrow", None), P("wide", "narrow", None)),
        check_vma=False,
    )
```
